256 devices in a mesh: energy: 16 (over x_lo, z), slab: 16 (over y, x_hi, core).
Axes of the slice: x: 4 (x_hi: 2, x_lo: 2; x = x_hi * 2 + x_lo), y: 4, z: 8, core: 2. Of those that a mesh axis runs over, the one named last changes fastest.
Arguments:
- onsite: float32 [16, 256], P('slab'), may hold values from -1 to 1
- hopping: float32 [16, 256, 256], P('slab'), may hold values from -0.12 to 0.12
- coupling: float32 [16, 256], P('slab'), may hold values from 0.4 to 0.8
- boundary_green: float32 [2, 16, 32, 256, 256], P(None, 'slab', 'energy'), may hold values from -0.09 to 0.09
- damping: float32 [16, 32], P('slab', 'energy'), may hold values from 1.5 to 6
- occupation: float32 [16, 32], P('slab', 'energy'), may hold values from 0 to 1
- tile_map: int32 [16, 128, 128], P('slab'), may hold values from 0 to 255
- prev_potential: float32 [16, 128, 128], P('slab'), may hold values from -6 to 6
Outputs:
- lesser_diag: float32 [16, 32, 256], P('slab', 'energy')
- potential: float32 [16, 128, 128], P('slab', 'energy')
The draws below stay inside these ranges and needn't reach their ends.
All inputs are finite; a program needn't handle non-finite values.
Results may differ from the reference program's by a relative error of at most 0.0003.
Values sent between devices are 32-bit elements; how exact they have to be, the bound alone decides.
A program may use at most 64 MiB of HBM per device.

```python
import math
import jax
import jax.numpy as jnp
from jax import lax

ORB = 256
GY = 128
GZ = 128
SHIFT = 2
NS_ITERS = 3
SWEEPS = 2
NSLAB = 16
NE = 32


def place_ends(drawn, rng, least, top_value):
    shape = drawn.shape
    place = [jax.random.randint(jax.random.fold_in(rng, axis), (), 0, shape[axis]) for axis in range(len(shape))]
    drawn = drawn.at[tuple(place)].set(least)
    longest = shape.index(max(shape))
    place[longest] = (place[longest] + 1) % shape[longest]
    return drawn.at[tuple(place)].set(top_value)


def level_of(key, dims, shards, least, largest):
    gain, own = 1.0, jax.random.fold_in(key, 6)
    for axis_at, parts in shards:
        steps = jnp.exp(jax.random.uniform(jax.random.fold_in(own, axis_at), (parts,), jnp.float32, least / len(shards), largest / len(shards)))
        gain = gain * jnp.repeat(steps, dims[axis_at] // parts).reshape([-1 if axis == axis_at else 1 for axis in range(len(dims))])
    return gain


def bell_draw(stream_key, dims, scale, most, shards=(), kind=jnp.bfloat16):
    result = jax.random.normal(stream_key, dims, jnp.float32) * scale
    if len(shards) > 0:
        result = level_of(stream_key, dims, shards, -0.22, 0.18) * result
    return jnp.clip(result, min=-most, max=most).astype(kind)


def setup_inputs(seed: int = 0) -> dict:
    splits = jax.random.split(jax.random.key(seed), 9)
    return {
        "onsite": jnp.clip(jax.random.uniform(splits[0], (NSLAB, ORB), jnp.float32, -1.0, 1.0) * level_of(splits[0], (NSLAB, ORB), ((0, 16),), -0.4, 0.0), -1.0, 1.0),
        "hopping": bell_draw(splits[1], (NSLAB, ORB, ORB), 0.02, 0.12, ((0, 16),), jnp.float32),
        "coupling": jnp.clip(0.4 + 0.4 * jax.random.uniform(splits[2], (NSLAB, ORB), jnp.float32) ** level_of(splits[2], (NSLAB, ORB), ((0, 16),), -0.2, 0.2), 0.4, 0.8),
        "boundary_green": bell_draw(splits[3], (2, NSLAB, NE, ORB, ORB), 0.015, 0.09, ((1, 16), (2, 16)), jnp.float32),
        "damping": jnp.clip(jnp.exp(math.log(6.0) - 1.3862944 * jax.random.uniform(splits[4], (NSLAB, NE), jnp.float32) ** level_of(splits[4], (NSLAB, NE), ((0, 16), (1, 16)), -0.2, 0.2)), 1.5, 6.0),
        "occupation": jnp.clip(1.0 * jax.random.uniform(splits[5], (NSLAB, NE), jnp.float32) ** level_of(splits[5], (NSLAB, NE), ((0, 16), (1, 16)), -0.2, 0.2), 0.0, 1.0),
        "tile_map": place_ends(jax.random.randint(splits[6], (NSLAB, GY, GZ), 0, ORB), jax.random.fold_in(splits[6], 1), 0, ORB - 1).astype(jnp.int32),
        "prev_potential": bell_draw(splits[7], (NSLAB, GY, GZ), 1.0, 6.0, ((0, 16),), jnp.float32),
    }


HIGHEST = lax.Precision.HIGHEST
PHONON = 0.5
CHARGE = 2.0
ANISO = 0.05
SCREEN = 0.05


def matmul_complex(left, right):
    def real_product(first, second):
        return jnp.einsum("...ij,...jk->...ik", first, second, precision=HIGHEST)
    return jnp.stack([real_product(left[0], right[0]) - real_product(left[1], right[1]),
                      real_product(left[0], right[1]) + real_product(left[1], right[0])])


def adjoint(matrix):
    return jnp.stack([jnp.swapaxes(matrix[0], -1, -2), -jnp.swapaxes(matrix[1], -1, -2)])


def invert(system, inverse_real, inverse_imag):
    unit_matrix = jnp.eye(system.shape[-1], dtype=jnp.float32)
    approx = jnp.stack([inverse_real[..., None] * unit_matrix, inverse_imag[..., None] * unit_matrix])
    for iteration in range(NS_ITERS):
        product = matmul_complex(system, approx)
        correction = jnp.stack([2.0 * unit_matrix - product[0], -product[1]])
        approx = matmul_complex(approx, correction)
    return approx


def spread_density(density, index_map):
    row_count, column_count = index_map.shape
    block_rows = math.gcd(row_count, 8)
    blocks = index_map.reshape(row_count // block_rows, block_rows, column_count)
    orbitals = jnp.arange(density.shape[0], dtype=jnp.int32)

    def one_block(indices):
        onehot = (indices[..., None] == orbitals).astype(jnp.float32)
        return jnp.einsum("bcn,n->bc", onehot, density, precision=HIGHEST)
    return lax.map(one_block, blocks).reshape(row_count, column_count)


def slab_spectrum(hopping_block, onsite_row, left_green, right_green, left_coupling, self_coupling, damping_row, occupation_row, energies):
    weight_left = left_coupling[:, None] * left_coupling[None, :]
    weight_self = self_coupling[:, None] * self_coupling[None, :]
    self_energy = weight_left * left_green + weight_self * right_green
    diag_real = energies[:, None] - onsite_row[None, :]
    diag_imag = damping_row[:, None] * jnp.ones_like(onsite_row)[None, :]
    modulus = diag_real * diag_real + diag_imag * diag_imag
    inverse_real = diag_real / modulus
    inverse_imag = -diag_imag / modulus
    unit_matrix = jnp.eye(onsite_row.shape[0], dtype=jnp.float32)
    system = jnp.stack([diag_real[..., None] * unit_matrix - hopping_block[None] - self_energy[0],
                        diag_imag[..., None] * unit_matrix - self_energy[1]])
    green_first = invert(system, inverse_real, inverse_imag)
    sigma_less = -occupation_row[None, :, None, None] * (self_energy - adjoint(self_energy))
    lesser_first = matmul_complex(matmul_complex(green_first, sigma_less), adjoint(green_first))
    widths = ((0, 0), (SHIFT, SHIFT), (0, 0), (0, 0))
    wide_green = jnp.pad(green_first, widths)
    wide_less = jnp.pad(lesser_first, widths)
    count = energies.shape[0]
    phonon_green = PHONON * (wide_green[:, :count] + wide_green[:, 2 * SHIFT:])
    phonon_less = PHONON * (wide_less[:, :count] + wide_less[:, 2 * SHIFT:])
    green_second = invert(system - phonon_green, inverse_real, inverse_imag)
    mixed_block = matmul_complex(green_second, sigma_less + phonon_less)
    return jnp.sum(mixed_block[1] * green_second[0] - mixed_block[0] * green_second[1], axis=-1)


def line_solve(right_side, main_diagonal):
    def forward(carry, plane):
        pivot_prev, eliminated_prev = carry
        pivot = main_diagonal - 1.0 / pivot_prev
        factor = main_diagonal - pivot
        eliminated = plane + factor * eliminated_prev
        return (pivot, eliminated), (pivot, eliminated)

    start = (jnp.float32(jnp.inf), jnp.zeros_like(right_side[0]))
    unused, (pivots, eliminated) = lax.scan(forward, start, right_side)

    def backward(after, inputs):
        pivot, plane = inputs
        inverse_pivot = 1.0 / pivot
        value = inverse_pivot * after + plane * inverse_pivot
        return value, value

    unused_last, solved = lax.scan(backward, jnp.zeros_like(right_side[0]), (pivots, eliminated), reverse=True)
    return solved


def reference(onsite, hopping, coupling, boundary_green, damping, occupation, tile_map, prev_potential):
    energies = -2.0 + 4.0 * (jnp.arange(NE, dtype=jnp.int32).astype(jnp.float32) + 0.5) / NE
    green_slabs = jnp.moveaxis(boundary_green, 1, 0)
    zero_slab = jnp.zeros_like(green_slabs[:1])
    left_greens = jnp.concatenate([zero_slab, green_slabs[:-1]], axis=0)
    right_greens = jnp.concatenate([green_slabs[1:], zero_slab], axis=0)
    left_couplings = jnp.concatenate([jnp.zeros_like(coupling[:1]), coupling[:-1]], axis=0)

    def one_slab(inputs):
        hopping_block, onsite_row, left_green, right_green, left_coupling, self_coupling, damping_row, occupation_row = inputs
        return slab_spectrum(hopping_block, onsite_row, left_green, right_green, left_coupling, self_coupling, damping_row, occupation_row, energies)

    lesser_diag = lax.map(one_slab, (hopping, onsite, left_greens, right_greens, left_couplings, coupling, damping, occupation))
    density = (4.0 / NE) * jnp.sum(lesser_diag, axis=1)
    source = CHARGE * lax.map(lambda pair: spread_density(pair[0], pair[1]), (density, tile_map))
    main_diagonal = 2.0 + 4.0 * ANISO + SCREEN
    potential = prev_potential
    for sweep_index in range(SWEEPS):
        padded = jnp.pad(potential, ((0, 0), (1, 1), (1, 1)))
        beside = padded[:, 2:, 1:-1] + padded[:, :-2, 1:-1] + padded[:, 1:-1, 2:] + padded[:, 1:-1, :-2]
        potential = line_solve(source + ANISO * beside, main_diagonal)
    return lesser_diag, potential
```

```python
import functools

import jax
import jax.numpy as jnp
import numpy as np
from jax import lax
from jax.experimental import pallas as pl
from jax.experimental.pallas import tpu as pltpu
from jax.sharding import PartitionSpec as P

F32 = jnp.float32
BF16 = jnp.bfloat16
MESH = pl.DeviceIdType.MESH
PHONON = 0.5
CHARGE = 2.0
ANISO = 0.05
SCREEN = 0.05
ROWS = 64


def line_tables(count):
    main = 2.0 + 4.0 * ANISO + SCREEN
    matrix = main * np.eye(count) - np.eye(count, k=1) - np.eye(count, k=-1)
    inverse = np.linalg.inv(matrix)
    around = (np.arange(count)[:, None] + np.arange(count)[None, :]) % count
    rows = np.arange(count)[:, None]
    return np.stack([inverse[rows, around], (inverse @ inverse)[rows, around]]).astype(np.float32)


def halves(value):
    high = value.astype(BF16)
    return high, (value - high.astype(F32)).astype(BF16)


def split(real, imag):
    return halves(real), halves(imag), halves(real + imag)


def times(first, second, turned):
    contract = (((1,), (1,)), ((), ())) if turned else (((1,), (0,)), ((), ()))

    def dot(a, b):
        return lax.dot_general(a, b, contract, preferred_element_type=F32)

    return dot(first[0], second[0]) + dot(first[0], second[1]) + dot(first[1], second[0])


def product(left, right, turned=False):
    one = times(left[0], right[0], turned)
    two = times(left[1], right[1], turned)
    both = times(left[2], right[2], turned)
    return one - two, both - one - two


def born_kernel(
    axis_sizes,
    green,
    hopping,
    onsite,
    coupling,
    damping,
    occupation,
    out,
    from_left,
    from_right,
    self_energy,
    facts,
    columns,
    block,
    phonon,
    slab_send,
    slab_recv,
    energy_send,
    energy_recv,
    fact_send,
    fact_recv,
):
    energies, slabs = axis_sizes
    e, s = lax.axis_index("energy"), lax.axis_index("slab")
    here = hopping.shape[-1]
    chunks = here // ROWS
    owned = 2
    has = {
        "left": s > 0,
        "right": s < slabs - 1,
        "below": e > 0,
        "above": e < energies - 1,
    }
    device = {"left": (e, s - 1), "right": (e, s + 1), "below": (e - 1, s), "above": (e + 1, s)}

    facts[3, 0:1, :] = coupling[...]
    for k in range(owned):
        facts[3, 1 + k : 2 + k, :] = jnp.full((1, here), damping[0, k], F32)
        facts[3, 3 + k : 4 + k, :] = jnp.full((1, here), occupation[0, k], F32)

    barrier = pltpu.get_barrier_semaphore()
    for side in ("left", "right", "below", "above"):

        @pl.when(has[side])
        def _():
            pl.semaphore_signal(barrier, inc=1, device_id=device[side], device_id_type=MESH)

    pl.semaphore_wait(barrier, sum(has[side].astype(jnp.int32) for side in has))

    def slab_copy(side, c):
        k, row = c // chunks, pl.multiple_of(lax.rem(c, chunks) * ROWS, ROWS)
        index = 0 if side == "right" else 1
        landing = from_left if side == "right" else from_right
        return pltpu.make_async_remote_copy(
            src_ref=green.at[:, 0, k, pl.ds(row, ROWS), :],
            dst_ref=landing.at[c],
            send_sem=slab_send.at[index, c],
            recv_sem=slab_recv.at[index, c],
            device_id=device[side],
            device_id_type=MESH,
        )

    def energy_copy(side, c):
        k, row = c // chunks, pl.multiple_of(lax.rem(c, chunks) * ROWS, ROWS)
        index = 0 if side == "above" else 1
        return pltpu.make_async_remote_copy(
            src_ref=self_energy.at[0, k, :, pl.ds(row, ROWS), :],
            dst_ref=self_energy.at[1 + index, k, :, pl.ds(row, ROWS), :],
            send_sem=energy_send.at[index, c],
            recv_sem=energy_recv.at[index, c],
            device_id=device[side],
            device_id_type=MESH,
        )

    def fact_copy(side):
        index = {"right": 0, "above": 1, "below": 2}[side]
        return pltpu.make_async_remote_copy(
            src_ref=facts.at[3],
            dst_ref=facts.at[index],
            send_sem=fact_send.at[index],
            recv_sem=fact_recv.at[index],
            device_id=device[side],
            device_id_type=MESH,
        )

    @pl.when(has["right"])
    def _():
        fact_copy("right").start()

    def send_green(c, carry):
        @pl.when(has["right"])
        def _():
            slab_copy("right", c).start()

        @pl.when(has["left"])
        def _():
            slab_copy("left", c).start()

        return carry

    lax.fori_loop(0, owned * chunks, send_green, 0)

    for side in ("above", "below"):

        @pl.when(has[side])
        def _():
            fact_copy(side).start()

    rows = lax.broadcasted_iota(jnp.int32, (here, here), 0)
    lanes = lax.broadcasted_iota(jnp.int32, (here, here), 1)

    def column(row):
        return jnp.sum(jnp.where(rows == lanes, row, 0.0), axis=1, keepdims=True)

    columns[:, 0:1] = column(onsite[...])
    columns[:, 1:2] = column(coupling[...])

    @pl.when(jnp.logical_not(has["left"]))
    def _():
        from_left[...] = jnp.zeros_like(from_left)
        facts[0] = jnp.zeros_like(facts[0])

    @pl.when(jnp.logical_not(has["right"]))
    def _():
        from_right[...] = jnp.zeros_like(from_right)

    @pl.when(has["left"])
    def _():
        fact_copy("right").wait_recv()

    columns[:, 2:3] = column(facts[0, 0:1, :])

    def form_self_energy(c, carry):
        k, row = c // chunks, pl.multiple_of(lax.rem(c, chunks) * ROWS, ROWS)

        @pl.when(has["left"])
        def _():
            slab_copy("right", c).wait_recv()

        @pl.when(has["right"])
        def _():
            slab_copy("left", c).wait_recv()

        weight_left = columns[pl.ds(row, ROWS), 2:3] * facts[0, 0:1, :]
        weight_right = columns[pl.ds(row, ROWS), 1:2] * facts[3, 0:1, :]
        for part in range(2):
            self_energy[0, k, part, pl.ds(row, ROWS), :] = (
                weight_left * from_left[c, part] + weight_right * from_right[c, part]
            )
        for side in ("above", "below"):

            @pl.when(has[side])
            def _():
                energy_copy(side, c).start()

        return carry

    def diagonal_inverse(energy, level, damp):
        real = energy - level
        modulus = real * real + damp * damp
        return real / modulus, -damp / modulus

    def step(t, carry):
        k, kind = t // 3, lax.rem(t, 3)
        lax.fori_loop(
            jnp.where(t == 0, 0, jnp.minimum(owned * chunks - 3 + t, owned * chunks)),
            jnp.minimum(owned * chunks - 2 + t, owned * chunks),
            form_self_energy,
            0,
        )
        slot = jnp.where(kind == 2, 0, 1 + kind)
        fact = jnp.where(kind == 2, 3, 1 + kind)
        present = jnp.where(kind == 0, e, jnp.where(kind == 1, energies - 1 - e, 1)) > 0

        def arrive(side):
            def one(c, inner):
                energy_copy(side, c).wait_recv()
                return inner

            lax.fori_loop(k * chunks, (k + 1) * chunks, one, 0)

            @pl.when(k == 0)
            def _():
                fact_copy(side).wait_recv()

        @pl.when((kind == 0) & has["below"])
        def _():
            arrive("above")

        @pl.when((kind == 1) & has["above"])
        def _():
            arrive("below")

        @pl.when(kind == 0)
        def _():
            phonon[...] = jnp.zeros_like(phonon)

        @pl.when(present)
        def _():
            place = owned * (e + jnp.where(kind == 2, 0, 2 * kind - 1)) + k
            energy = -2.0 + 4.0 * (place.astype(F32) + 0.5) / (owned * energies)
            damp = facts[fact, pl.ds(1 + k, 1), :]
            x_real, x_imag = diagonal_inverse(energy, onsite[...], damp)
            se_real, se_imag = self_energy[slot, k, 0], self_energy[slot, k, 1]

            @pl.when(kind < 2)
            def _():
                block[0] = hopping[0] + se_real
                block[1] = se_imag

            @pl.when(kind == 2)
            def _():
                block[0] = hopping[0] + se_real + phonon[0]
                block[1] = se_imag + phonon[1]

            h_real, h_imag = block[0], block[1]
            a_real = h_real * x_real - h_imag * x_imag
            a_imag = h_real * x_imag + h_imag * x_real
            a = split(a_real, a_imag)
            square = product(a, a)
            two = split(*square)
            cube = product(a, two)
            fourth = product(two, two)
            t_real = a_real + square[0] + cube[0]
            t_imag = a_imag + square[1] + cube[1]
            rest = product(split(t_real, t_imag), split(*fourth))
            t_real = t_real + fourth[0] + rest[0]
            t_imag = t_imag + fourth[1] + rest[1]
            series = split(t_real, t_imag)

            fill = facts[fact, pl.ds(3 + k, 1), :]
            sigma_real = -fill * (se_real - se_real.T)
            sigma_imag = -fill * (se_imag + se_imag.T)

            @pl.when(kind < 2)
            def _():
                more = product(series, split(sigma_real, sigma_imag))
                w_real, w_imag = sigma_real + more[0], sigma_imag + more[1]
                adjoint = (series[0], halves(-t_imag), halves(t_real - t_imag))
                more = product(split(w_real, w_imag), adjoint, True)
                u_real, u_imag = w_real + more[0], w_imag + more[1]
                c_real, c_imag = diagonal_inverse(energy, columns[:, 0:1], damp[:, 0:1])
                c_real, c_imag = PHONON * c_real, PHONON * c_imag
                v_real = c_real * u_real - c_imag * u_imag
                v_imag = c_real * u_imag + c_imag * u_real
                unit = jnp.where(rows == lanes, 1.0, 0.0)
                g_real = unit + t_real
                phonon[0] += c_real * g_real - c_imag * t_imag
                phonon[1] += c_real * t_imag + c_imag * g_real
                phonon[2] += v_real * x_real + v_imag * x_imag
                phonon[3] += v_imag * x_real - v_real * x_imag

            @pl.when(kind == 2)
            def _():
                mixed_real = sigma_real + phonon[2]
                mixed_imag = sigma_imag + phonon[3]
                more = product(series, split(mixed_real, mixed_imag))
                w_real, w_imag = mixed_real + more[0], mixed_imag + more[1]
                terms = w_imag * t_real - w_real * t_imag + jnp.where(rows == lanes, w_imag, 0.0)
                total = jnp.sum(terms.T, axis=0, keepdims=True)
                out[pl.ds(k, 1), :] = (x_real * x_real + x_imag * x_imag) * total

        return carry

    lax.fori_loop(0, 3 * owned, step, 0)

    def settle(c, carry):
        for side in ("right", "left"):

            @pl.when(has[side])
            def _():
                slab_copy(side, c).wait_send()

        for side in ("above", "below"):

            @pl.when(has[side])
            def _():
                energy_copy(side, c).wait_send()

        return carry

    lax.fori_loop(0, owned * chunks, settle, 0)
    for side in ("right", "above", "below"):

        @pl.when(has[side])
        def _():
            fact_copy(side).wait_send()


def born(axis_sizes, green, hopping, onsite, coupling, damping, occupation):
    size = hopping.shape[-1]
    count = 2 * (size // ROWS)
    vmem, smem = pl.BlockSpec(memory_space=pltpu.VMEM), pl.BlockSpec(memory_space=pltpu.SMEM)
    return pl.pallas_call(
        functools.partial(born_kernel, axis_sizes),
        out_shape=jax.ShapeDtypeStruct((2, size), F32),
        in_specs=[pl.BlockSpec(memory_space=pl.ANY), vmem, vmem, vmem, smem, smem],
        out_specs=vmem,
        scratch_shapes=[
            pltpu.VMEM((count, 2, ROWS, size), F32),
            pltpu.VMEM((count, 2, ROWS, size), F32),
            pltpu.VMEM((3, 2, 2, size, size), F32),
            pltpu.VMEM((4, 8, size), F32),
            pltpu.VMEM((size, 128), F32),
            pltpu.VMEM((2, size, size), F32),
            pltpu.VMEM((4, size, size), F32),
            pltpu.SemaphoreType.DMA((2, count)),
            pltpu.SemaphoreType.DMA((2, count)),
            pltpu.SemaphoreType.DMA((2, count)),
            pltpu.SemaphoreType.DMA((2, count)),
            pltpu.SemaphoreType.DMA((3,)),
            pltpu.SemaphoreType.DMA((3,)),
        ],
        compiler_params=pltpu.CompilerParams(
            collective_id=0, has_side_effects=True, vmem_limit_bytes=50 << 20
        ),
        name="born",
    )(green, hopping, onsite, coupling, damping, occupation)


def poisson_kernel(
    axis_sizes,
    lesser,
    tile_map,
    previous,
    tables,
    out,
    densities,
    weighted,
    landed,
    density_send,
    density_recv,
    plane_send,
    plane_recv,
):
    energies, slabs = axis_sizes
    e, s = lax.axis_index("energy"), lax.axis_index("slab")
    rows = out.shape[1]
    width = out.shape[2]
    barrier = pltpu.get_barrier_semaphore()
    for d in range(1, energies):
        pl.semaphore_signal(
            barrier, inc=1, device_id=(lax.rem(e + d, energies), s), device_id_type=MESH
        )
    for d in range(1, slabs):
        pl.semaphore_signal(
            barrier, inc=1, device_id=(e, lax.rem(s + d, slabs)), device_id_type=MESH
        )
    densities[e] = (4.0 / (2 * energies)) * jnp.sum(lesser[...], axis=0, keepdims=True)
    pl.semaphore_wait(barrier, energies + slabs - 2)

    def density_copy(d):
        return pltpu.make_async_remote_copy(
            src_ref=densities.at[e],
            dst_ref=densities.at[e],
            send_sem=density_send.at[d],
            recv_sem=density_recv.at[d],
            device_id=(lax.rem(e + d, energies), s),
            device_id_type=MESH,
        )

    def density_landing(d):
        slot = lax.rem(e + energies - d, energies)
        return pltpu.make_async_remote_copy(
            src_ref=densities.at[slot],
            dst_ref=densities.at[slot],
            send_sem=density_send.at[d],
            recv_sem=density_recv.at[d],
            device_id=(lax.rem(e + d, energies), s),
            device_id_type=MESH,
        )

    def plane_copy(d):
        return pltpu.make_async_remote_copy(
            src_ref=weighted.at[d],
            dst_ref=landed.at[d],
            send_sem=plane_send.at[d],
            recv_sem=plane_recv.at[d],
            device_id=(e, lax.rem(s + d, slabs)),
            device_id_type=MESH,
        )

    for d in range(1, energies):
        density_copy(d).start()

    def blocks(ref):
        own = ref[0, pl.ds(pl.multiple_of(e * rows, rows), rows), :]
        before = ref[0, pl.ds(pl.multiple_of(jnp.maximum(e - 1, 0) * rows, rows), rows), :]
        after = ref[
            0, pl.ds(pl.multiple_of(jnp.minimum(e + 1, energies - 1) * rows, rows), rows), :
        ]
        return before, own, after

    lane = lax.broadcasted_iota(jnp.int32, (3 * rows, width), 1)
    line = lax.broadcasted_iota(jnp.int32, (3 * rows, width), 0) + (e - 1) * rows
    inside = (line >= 0) & (line < energies * rows)

    def beside(field):
        up = pltpu.roll(field, 1, 0)
        down = pltpu.roll(field, 3 * rows - 1, 0)
        left = jnp.where(lane == 0, 0.0, pltpu.roll(field, 1, 1))
        right = jnp.where(lane == width - 1, 0.0, pltpu.roll(field, width - 1, 1))
        return up + down + left + right

    potential = jnp.where(inside, jnp.concatenate(blocks(previous), axis=0), 0.0)
    potential = jnp.where(inside, beside(potential), 0.0)
    potential = (ANISO * ANISO) * beside(potential)[rows : 2 * rows]
    index = jnp.concatenate(blocks(tile_map), axis=0)

    for d in range(1, energies):
        density_landing(d).wait_recv()
    density = CHARGE * jnp.sum(densities[...], axis=0)

    def spread(half):
        table = jnp.broadcast_to(density[:, half * width : (half + 1) * width], (3 * rows, width))
        return jnp.take_along_axis(table, index & (width - 1), axis=1)

    source = jnp.where(inside, jnp.where(index < width, spread(0), spread(1)), 0.0)
    second = ANISO * beside(source)[rows : 2 * rows] + potential
    source = source[rows : 2 * rows]
    for d in range(1, slabs):
        weighted[d] = tables[0, s, d] * source + tables[1, s, d] * second
        plane_copy(d).start()
    total = tables[0, s, 0] * source + tables[1, s, 0] * second
    for d in range(1, slabs):
        plane_copy(d).wait_recv()
        total = total + landed[d]
    out[0] = total
    for d in range(1, energies):
        density_copy(d).wait_send()
    for d in range(1, slabs):
        plane_copy(d).wait_send()


def poisson(axis_sizes, lesser, tile_map, previous, tables):
    energies, slabs = axis_sizes
    rows, width = tile_map.shape[1] // energies, tile_map.shape[2]
    vmem, smem = pl.BlockSpec(memory_space=pltpu.VMEM), pl.BlockSpec(memory_space=pltpu.SMEM)
    return pl.pallas_call(
        functools.partial(poisson_kernel, axis_sizes),
        out_shape=jax.ShapeDtypeStruct((1, rows, width), F32),
        in_specs=[vmem, vmem, vmem, smem],
        out_specs=vmem,
        scratch_shapes=[
            pltpu.VMEM((energies, 1, lesser.shape[1]), F32),
            pltpu.VMEM((slabs, rows, width), F32),
            pltpu.VMEM((slabs, rows, width), F32),
            pltpu.SemaphoreType.DMA((energies,)),
            pltpu.SemaphoreType.DMA((energies,)),
            pltpu.SemaphoreType.DMA((slabs,)),
            pltpu.SemaphoreType.DMA((slabs,)),
        ],
        compiler_params=pltpu.CompilerParams(
            collective_id=1, has_side_effects=True, vmem_limit_bytes=16 << 20
        ),
        name="poisson",
    )(lesser, tile_map, previous, tables)


def solution(mesh):
    axis_sizes = (mesh.shape["energy"], mesh.shape["slab"])
    tables = line_tables(axis_sizes[1])

    def per_device(onsite, hopping, coupling, green, damping, occupation, tile_map, previous):
        lesser = born(axis_sizes, green, hopping, onsite, coupling, damping, occupation)
        potential = poisson(axis_sizes, lesser, tile_map, previous, jnp.asarray(tables))
        return lesser[None], potential

    in_specs = (
        P("slab", None),
        P("slab", None, None),
        P("slab", None),
        P(None, "slab", "energy", None, None),
        P("slab", "energy"),
        P("slab", "energy"),
        P("slab", None, None),
        P("slab", None, None),
    )
    out_specs = (P("slab", "energy", None), P("slab", "energy", None))
    return jax.shard_map(
        per_device, mesh=mesh, in_specs=in_specs, out_specs=out_specs, check_vma=False
    )
```

```python
import functools

import jax
import jax.numpy as jnp
import numpy as np
from jax import lax
from jax.experimental import pallas as pl
from jax.experimental.pallas import tpu as pltpu
from jax.sharding import PartitionSpec as P

F32 = jnp.float32
BF16 = jnp.bfloat16
MESH = pl.DeviceIdType.MESH
PHONON = 0.5
CHARGE = 2.0
ANISO = 0.05
SCREEN = 0.05
ROWS = 32


def line_tables(count):
    main = 2.0 + 4.0 * ANISO + SCREEN
    matrix = main * np.eye(count) - np.eye(count, k=1) - np.eye(count, k=-1)
    inverse = np.linalg.inv(matrix)
    around = (np.arange(count)[:, None] + np.arange(count)[None, :]) % count
    rows = np.arange(count)[:, None]
    weights = np.stack([inverse[rows, around], (inverse @ inverse)[rows, around]], axis=-1)
    return np.repeat(weights[..., None], 128, axis=-1).astype(np.float32)


def halves(value):
    high = value.astype(BF16)
    return high, (value - high.astype(F32)).astype(BF16)


def split(real, imag):
    return halves(real), halves(imag), halves(real + imag)


def times(first, second, turned):
    contract = (((1,), (1,)), ((), ())) if turned else (((1,), (0,)), ((), ()))

    def dot(a, b):
        return lax.dot_general(a, b, contract, preferred_element_type=F32)

    return dot(first[0], second[0]) + dot(first[0], second[1]) + dot(first[1], second[0])


def product(left, right, turned=False):
    one = times(left[0], right[0], turned)
    two = times(left[1], right[1], turned)
    both = times(left[2], right[2], turned)
    return one - two, both - one - two


def step_kernel(
    axis_sizes,
    green,
    hopping_hbm,
    onsite_hbm,
    coupling_hbm,
    damping_hbm,
    occupation_hbm,
    tile_map_hbm,
    previous_hbm,
    tables_hbm,
    out,
    potential_out,
    hopping,
    onsite,
    coupling,
    damping,
    occupation,
    tile_map,
    previous,
    tables,
    load,
    from_left,
    from_right,
    self_energy,
    relay,
    facts,
    columns,
    block,
    phonon,
    stencil,
    densities,
    weighted,
    landed,
    slab_send,
    slab_recv,
    energy_send,
    energy_recv,
    relay_recv,
    forward_send,
    fact_send,
    fact_recv,
    density_send,
    density_recv,
    plane_send,
    plane_recv,
):
    energies, slabs = axis_sizes
    e, s = lax.axis_index("energy"), lax.axis_index("slab")
    here = hopping.shape[-1]
    chunks = here // ROWS
    owned = 2
    half = energies // 2
    has = {
        "left": s > 0,
        "right": s < slabs - 1,
        "below": e > 0,
        "above": e < energies - 1,
    }
    device = {"left": (e, s - 1), "right": (e, s + 1), "below": (e - 1, s), "above": (e + 1, s)}
    crosses = {"above": e == half - 1, "below": e == half}
    relays = (e == 0) | (e == energies - 1)

    barrier = pltpu.get_barrier_semaphore()
    for d in range(1, energies):
        pl.semaphore_signal(
            barrier, inc=1, device_id=(lax.rem(e + d, energies), s), device_id_type=MESH
        )
    for d in range(1, slabs):
        pl.semaphore_signal(
            barrier, inc=1, device_id=(e, lax.rem(s + d, slabs)), device_id_type=MESH
        )

    def loads():
        pairs = (
            (coupling_hbm, coupling),
            (damping_hbm, damping),
            (occupation_hbm, occupation),
            (onsite_hbm, onsite),
            (previous_hbm, previous),
            (tile_map_hbm, tile_map),
            (hopping_hbm, hopping),
            (tables_hbm.at[s], tables),
        )
        return [pltpu.make_async_copy(a, b, load.at[i]) for i, (a, b) in enumerate(pairs)]

    for copy in loads():
        copy.start()
    for copy in loads():
        copy.wait()

    facts[3, 0:1, :] = coupling[...]
    for k in range(owned):
        facts[3, 1 + k : 2 + k, :] = jnp.broadcast_to(damping[:, k : k + 1], (1, here))
        facts[3, 3 + k : 4 + k, :] = jnp.broadcast_to(occupation[:, k : k + 1], (1, here))

    pl.semaphore_wait(barrier, energies + slabs - 2)

    def slab_copy(side, c):
        k, row = c // chunks, pl.multiple_of(lax.rem(c, chunks) * ROWS, ROWS)
        index = 0 if side == "right" else 1
        landing = from_left if side == "right" else from_right
        return pltpu.make_async_remote_copy(
            src_ref=green.at[:, 0, k, pl.ds(row, ROWS), :],
            dst_ref=landing.at[c],
            send_sem=slab_send.at[index, c],
            recv_sem=slab_recv.at[index, c],
            device_id=device[side],
            device_id_type=MESH,
        )

    def energy_copy(side, c):
        k, row = c // chunks, pl.multiple_of(lax.rem(c, chunks) * ROWS, ROWS)
        index = 0 if side == "above" else 1
        return pltpu.make_async_remote_copy(
            src_ref=self_energy.at[0, k, :, pl.ds(row, ROWS), :],
            dst_ref=self_energy.at[1 + index, k, :, pl.ds(row, ROWS), :],
            send_sem=energy_send.at[index, c],
            recv_sem=energy_recv.at[index, c],
            device_id=device[side],
            device_id_type=MESH,
        )

    def relay_copy(side, c):
        k, row = c // chunks, pl.multiple_of(lax.rem(c, chunks) * ROWS, ROWS)
        index = 0 if side == "above" else 1
        return pltpu.make_async_remote_copy(
            src_ref=self_energy.at[0, k, :, pl.ds(row, ROWS), :],
            dst_ref=relay.at[c // 2],
            send_sem=energy_send.at[index, c],
            recv_sem=relay_recv.at[c // 2],
            device_id=(energies - 1 if side == "above" else 0, s),
            device_id_type=MESH,
        )

    def forward_copy(side, c):
        k, row = c // chunks, pl.multiple_of(lax.rem(c, chunks) * ROWS, ROWS)
        index = 0 if side == "above" else 1
        return pltpu.make_async_remote_copy(
            src_ref=relay.at[c // 2],
            dst_ref=self_energy.at[1 + index, k, :, pl.ds(row, ROWS), :],
            send_sem=forward_send.at[c // 2],
            recv_sem=energy_recv.at[index, c],
            device_id=(half if side == "above" else half - 1, s),
            device_id_type=MESH,
        )

    def forward(c):
        @pl.when(e == energies - 1)
        def _():
            relay_copy("above", c).wait_recv()
            forward_copy("above", c).start()

        @pl.when(e == 0)
        def _():
            relay_copy("below", c).wait_recv()
            forward_copy("below", c).start()

    def fact_copy(side):
        index = {"right": 0, "above": 1, "below": 2}[side]
        return pltpu.make_async_remote_copy(
            src_ref=facts.at[3],
            dst_ref=facts.at[index],
            send_sem=fact_send.at[index],
            recv_sem=fact_recv.at[index],
            device_id=device[side],
            device_id_type=MESH,
        )

    @pl.when(has["right"])
    def _():
        fact_copy("right").start()

    def send_green(c, carry):
        @pl.when(has["right"])
        def _():
            slab_copy("right", c).start()

        @pl.when(has["left"])
        def _():
            slab_copy("left", c).start()

        return carry

    lax.fori_loop(0, owned * chunks, send_green, 0)

    for side in ("above", "below"):

        @pl.when(has[side])
        def _():
            fact_copy(side).start()

    tall = potential_out.shape[1]
    width = potential_out.shape[2]

    def blocks(ref):
        own = ref[0, pl.ds(pl.multiple_of(e * tall, tall), tall), :]
        before = ref[0, pl.ds(pl.multiple_of(jnp.maximum(e - 1, 0) * tall, tall), tall), :]
        after = ref[
            0, pl.ds(pl.multiple_of(jnp.minimum(e + 1, energies - 1) * tall, tall), tall), :
        ]
        return before, own, after

    cell = lax.broadcasted_iota(jnp.int32, (3 * tall, width), 1)
    line = lax.broadcasted_iota(jnp.int32, (3 * tall, width), 0) + (e - 1) * tall
    inside = (line >= 0) & (line < energies * tall)

    def beside(field):
        up = pltpu.roll(field, 1, 0)
        down = pltpu.roll(field, 3 * tall - 1, 0)
        left = jnp.where(cell == 0, 0.0, pltpu.roll(field, 1, 1))
        right = jnp.where(cell == width - 1, 0.0, pltpu.roll(field, width - 1, 1))
        return up + down + left + right

    potential = jnp.where(inside, jnp.concatenate(blocks(previous), axis=0), 0.0)
    potential = jnp.where(inside, beside(potential), 0.0)
    stencil[...] = (ANISO * ANISO) * beside(potential)[tall : 2 * tall]

    rows = lax.broadcasted_iota(jnp.int32, (here, here), 0)
    lanes = lax.broadcasted_iota(jnp.int32, (here, here), 1)

    def column(row):
        return jnp.sum(jnp.where(rows == lanes, row, 0.0), axis=1, keepdims=True)

    columns[:, 0:1] = column(onsite[...])
    columns[:, 1:2] = column(coupling[...])

    @pl.when(jnp.logical_not(has["left"]))
    def _():
        from_left[...] = jnp.zeros_like(from_left)
        facts[0] = jnp.zeros_like(facts[0])

    @pl.when(jnp.logical_not(has["right"]))
    def _():
        from_right[...] = jnp.zeros_like(from_right)

    @pl.when(has["left"])
    def _():
        fact_copy("right").wait_recv()

    columns[:, 2:3] = column(facts[0, 0:1, :])

    def form_self_energy(c, carry):
        k, row = c // chunks, pl.multiple_of(lax.rem(c, chunks) * ROWS, ROWS)

        @pl.when(has["left"])
        def _():
            slab_copy("right", c).wait_recv()

        @pl.when(has["right"])
        def _():
            slab_copy("left", c).wait_recv()

        weight_left = columns[pl.ds(row, ROWS), 2:3] * facts[0, 0:1, :]
        weight_right = columns[pl.ds(row, ROWS), 1:2] * facts[3, 0:1, :]
        for part in range(2):
            self_energy[0, k, part, pl.ds(row, ROWS), :] = (
                weight_left * from_left[c, part] + weight_right * from_right[c, part]
            )
        for side in ("above", "below"):

            bent = crosses[side] & (lax.rem(c, 2) == 1)

            @pl.when(has[side] & jnp.logical_not(bent))
            def _():
                energy_copy(side, c).start()

            @pl.when(bent)
            def _():
                relay_copy(side, c).start()

        @pl.when((lax.rem(c, 2) == 1) & (c >= 3))
        def _():
            forward(c - 2)

        @pl.when(c == owned * chunks - 1)
        def _():
            forward(c)

        return carry

    def diagonal_inverse(energy, level, damp):
        real = energy - level
        modulus = real * real + damp * damp
        return real / modulus, -damp / modulus

    def step(t, carry):
        k, kind = t // 3, lax.rem(t, 3)
        lax.fori_loop(
            jnp.where(t == 0, 0, jnp.minimum(10 + 2 * t, owned * chunks)),
            jnp.minimum(12 + 2 * t, owned * chunks),
            form_self_energy,
            0,
        )
        side = jnp.where(lax.rem(e, half) >= half // 2, kind, 1 - kind)
        slot = jnp.where(kind == 2, 0, 1 + side)
        fact = jnp.where(kind == 2, 3, 1 + side)
        present = (kind == 2) | (jnp.where(side == 0, e, energies - 1 - e) > 0)

        def arrive(side):
            def one(c, inner):
                energy_copy(side, c).wait_recv()
                return inner

            lax.fori_loop(k * chunks, (k + 1) * chunks, one, 0)

            @pl.when(k == 0)
            def _():
                fact_copy(side).wait_recv()

        @pl.when((kind < 2) & (side == 0) & has["below"])
        def _():
            arrive("above")

        @pl.when((kind < 2) & (side == 1) & has["above"])
        def _():
            arrive("below")

        @pl.when(kind == 0)
        def _():
            phonon[...] = jnp.zeros_like(phonon)

        @pl.when(present)
        def _():
            place = owned * (e + jnp.where(kind == 2, 0, 2 * side - 1)) + k
            energy = -2.0 + 4.0 * (place.astype(F32) + 0.5) / (owned * energies)
            damp = facts[fact, pl.ds(1 + k, 1), :]
            x_real, x_imag = diagonal_inverse(energy, onsite[...], damp)
            se_real, se_imag = self_energy[slot, k, 0], self_energy[slot, k, 1]

            @pl.when(kind < 2)
            def _():
                block[0] = hopping[0] + se_real
                block[1] = se_imag

            @pl.when(kind == 2)
            def _():
                block[0] = hopping[0] + se_real + phonon[0]
                block[1] = se_imag + phonon[1]

            h_real, h_imag = block[0], block[1]
            a_real = h_real * x_real - h_imag * x_imag
            a_imag = h_real * x_imag + h_imag * x_real
            a = split(a_real, a_imag)
            square = product(a, a)
            two = split(*square)
            cube = product(a, two)
            fourth = product(two, two)
            t_real = a_real + square[0] + cube[0]
            t_imag = a_imag + square[1] + cube[1]
            rest = product(split(t_real, t_imag), split(*fourth))
            t_real = t_real + fourth[0] + rest[0]
            t_imag = t_imag + fourth[1] + rest[1]
            series = split(t_real, t_imag)

            fill = facts[fact, pl.ds(3 + k, 1), :]
            sigma_real = -fill * (se_real - se_real.T)
            sigma_imag = -fill * (se_imag + se_imag.T)

            @pl.when(kind < 2)
            def _():
                more = product(series, split(sigma_real, sigma_imag))
                w_real, w_imag = sigma_real + more[0], sigma_imag + more[1]
                adjoint = (series[0], halves(-t_imag), halves(t_real - t_imag))
                more = product(split(w_real, w_imag), adjoint, True)
                u_real, u_imag = w_real + more[0], w_imag + more[1]
                c_real, c_imag = diagonal_inverse(energy, columns[:, 0:1], damp[:, 0:1])
                c_real, c_imag = PHONON * c_real, PHONON * c_imag
                v_real = c_real * u_real - c_imag * u_imag
                v_imag = c_real * u_imag + c_imag * u_real
                unit = jnp.where(rows == lanes, 1.0, 0.0)
                g_real = unit + t_real
                phonon[0] += c_real * g_real - c_imag * t_imag
                phonon[1] += c_real * t_imag + c_imag * g_real
                phonon[2] += v_real * x_real + v_imag * x_imag
                phonon[3] += v_imag * x_real - v_real * x_imag

            @pl.when(kind == 2)
            def _():
                mixed_real = sigma_real + phonon[2]
                mixed_imag = sigma_imag + phonon[3]
                more = product(series, split(mixed_real, mixed_imag))
                w_real, w_imag = mixed_real + more[0], mixed_imag + more[1]
                terms = w_imag * t_real - w_real * t_imag + jnp.where(rows == lanes, w_imag, 0.0)
                total = jnp.sum(terms.T, axis=0, keepdims=True)
                out[pl.ds(k, 1), :] = (x_real * x_real + x_imag * x_imag) * total

        return carry

    lax.fori_loop(0, 3 * owned, step, 0)

    def settle(c, carry):
        for side in ("right", "left"):

            @pl.when(has[side])
            def _():
                slab_copy(side, c).wait_send()

        for side in ("above", "below"):

            @pl.when(has[side])
            def _():
                energy_copy(side, c).wait_send()

        @pl.when(relays & (lax.rem(c, 2) == 1))
        def _():
            forward_copy("above", c).wait_send()

        return carry

    def density_copy(d):
        return pltpu.make_async_remote_copy(
            src_ref=densities.at[e],
            dst_ref=densities.at[e],
            send_sem=density_send.at[d],
            recv_sem=density_recv.at[d],
            device_id=(lax.rem(e + d, energies), s),
            device_id_type=MESH,
        )

    def density_landing(d):
        slot = lax.rem(e + energies - d, energies)
        return pltpu.make_async_remote_copy(
            src_ref=densities.at[slot],
            dst_ref=densities.at[slot],
            send_sem=density_send.at[d],
            recv_sem=density_recv.at[d],
            device_id=(lax.rem(e + d, energies), s),
            device_id_type=MESH,
        )

    def plane_copy(d):
        return pltpu.make_async_remote_copy(
            src_ref=weighted.at[d],
            dst_ref=landed.at[d],
            send_sem=plane_send.at[d],
            recv_sem=plane_recv.at[d],
            device_id=(e, lax.rem(s + d, slabs)),
            device_id_type=MESH,
        )

    densities[e] = (4.0 / (owned * energies)) * jnp.sum(out[...], axis=0, keepdims=True)
    for d in range(1, energies):
        density_copy(d).start()
    for d in range(1, energies):
        density_landing(d).wait_recv()
    density = CHARGE * jnp.sum(densities[...], axis=0)

    index = jnp.concatenate(blocks(tile_map), axis=0)

    def spread(part):
        table = jnp.broadcast_to(density[:, part * width : (part + 1) * width], (3 * tall, width))
        return jnp.take_along_axis(table, index & (width - 1), axis=1)

    source = jnp.where(inside, jnp.where(index < width, spread(0), spread(1)), 0.0)
    second = ANISO * beside(source)[tall : 2 * tall] + stencil[...]
    source = source[tall : 2 * tall]
    for d in range(1, slabs):
        weighted[d] = tables[d, 0:1, :] * source + tables[d, 1:2, :] * second
        plane_copy(d).start()
    total = tables[0, 0:1, :] * source + tables[0, 1:2, :] * second
    for d in range(1, slabs):
        plane_copy(d).wait_recv()
        total = total + landed[d]
    potential_out[0] = total
    lax.fori_loop(0, owned * chunks, settle, 0)
    for side in ("right", "above", "below"):

        @pl.when(has[side])
        def _():
            fact_copy(side).wait_send()

    for d in range(1, energies):
        density_copy(d).wait_send()
    for d in range(1, slabs):
        plane_copy(d).wait_send()


def advance(axis_sizes, green, hopping, onsite, coupling, damping, occupation, tile_map, previous, tables):
    energies, slabs = axis_sizes
    size = hopping.shape[-1]
    count = 2 * (size // ROWS)
    tall, width = tile_map.shape[1] // energies, tile_map.shape[2]
    dma, vmem = pltpu.SemaphoreType.DMA, pl.BlockSpec(memory_space=pltpu.VMEM)
    local = (hopping, onsite, coupling, damping, occupation, tile_map, previous)
    return pl.pallas_call(
        functools.partial(step_kernel, axis_sizes),
        out_shape=(
            jax.ShapeDtypeStruct((2, size), F32),
            jax.ShapeDtypeStruct((1, tall, width), F32),
        ),
        in_specs=[pl.BlockSpec(memory_space=pl.ANY)] * 9,
        out_specs=(vmem, vmem),
        scratch_shapes=[
            *(pltpu.VMEM(array.shape, array.dtype) for array in local),
            pltpu.VMEM(tables.shape[1:], F32),
            dma((8,)),
            pltpu.VMEM((count, 2, ROWS, size), F32),
            pltpu.VMEM((count, 2, ROWS, size), F32),
            pltpu.VMEM((3, 2, 2, size, size), F32),
            pltpu.VMEM((count // 2, 2, ROWS, size), F32),
            pltpu.VMEM((4, 8, size), F32),
            pltpu.VMEM((size, 128), F32),
            pltpu.VMEM((2, size, size), F32),
            pltpu.VMEM((4, size, size), F32),
            pltpu.VMEM((tall, width), F32),
            pltpu.VMEM((energies, 1, size), F32),
            pltpu.VMEM((slabs, tall, width), F32),
            pltpu.VMEM((slabs, tall, width), F32),
            dma((2, count)),
            dma((2, count)),
            dma((2, count)),
            dma((2, count)),
            dma((count // 2,)),
            dma((count // 2,)),
            dma((3,)),
            dma((3,)),
            dma((energies,)),
            dma((energies,)),
            dma((slabs,)),
            dma((slabs,)),
        ],
        compiler_params=pltpu.CompilerParams(
            collective_id=0, has_side_effects=True, vmem_limit_bytes=60 << 20
        ),
        name="step",
    )(green, hopping, onsite, coupling, damping, occupation, tile_map, previous, tables)


def solution(mesh):
    axis_sizes = (mesh.shape["energy"], mesh.shape["slab"])
    tables = line_tables(axis_sizes[1])

    def per_device(onsite, hopping, coupling, green, damping, occupation, tile_map, previous):
        lesser, potential = advance(
            axis_sizes,
            green,
            hopping,
            onsite,
            coupling,
            damping,
            occupation,
            tile_map,
            previous,
            jnp.asarray(tables),
        )

        def finish(a, b, c, d):
            c[0] = a[...]
            d[...] = b[...]

        return tuple(
            pl.pallas_call(
                finish,
                out_shape=(
                    jax.ShapeDtypeStruct((1, *lesser.shape), F32),
                    jax.ShapeDtypeStruct(potential.shape, F32),
                ),
                name="finish",
            )(lesser, potential)
        )

    in_specs = (
        P("slab", None),
        P("slab", None, None),
        P("slab", None),
        P(None, "slab", "energy", None, None),
        P("slab", "energy"),
        P("slab", "energy"),
        P("slab", None, None),
        P("slab", None, None),
    )
    out_specs = (P("slab", "energy", None), P("slab", "energy", None))
    return jax.shard_map(
        per_device, mesh=mesh, in_specs=in_specs, out_specs=out_specs, check_vma=False
    )
```

```python
import functools

import jax
import jax.numpy as jnp
import numpy as np
from jax import lax
from jax.experimental import pallas as pl
from jax.experimental.pallas import tpu as pltpu
from jax.sharding import PartitionSpec as P

F32 = jnp.float32
BF16 = jnp.bfloat16
MESH = pl.DeviceIdType.MESH
PHONON = 0.5
CHARGE = 2.0
ANISO = 0.05
SCREEN = 0.05
LAG = 3
ROWS = 32


def line_tables(count):
    main = 2.0 + 4.0 * ANISO + SCREEN
    matrix = main * np.eye(count) - np.eye(count, k=1) - np.eye(count, k=-1)
    inverse = np.linalg.inv(matrix)
    around = (np.arange(count)[:, None] + np.arange(count)[None, :]) % count
    rows = np.arange(count)[:, None]
    weights = np.stack([inverse[rows, around], (inverse @ inverse)[rows, around]], axis=-1)
    return np.repeat(weights[..., None], 128, axis=-1).astype(np.float32)


def halves(value):
    high = value.astype(BF16)
    return high, (value - high.astype(F32)).astype(BF16)


def split(real, imag):
    return halves(real), halves(imag), halves(real + imag)


def times(first, second, turned):
    contract = (((1,), (1,)), ((), ())) if turned else (((1,), (0,)), ((), ()))

    def dot(a, b):
        return lax.dot_general(a, b, contract, preferred_element_type=F32)

    return dot(first[0], second[0]) + dot(first[0], second[1]) + dot(first[1], second[0])


def product(left, right, turned=False):
    one = times(left[0], right[0], turned)
    two = times(left[1], right[1], turned)
    both = times(left[2], right[2], turned)
    return one - two, both - one - two


def step_kernel(
    axis_sizes,
    green,
    hopping_hbm,
    onsite_hbm,
    coupling_hbm,
    damping_hbm,
    occupation_hbm,
    tile_map_hbm,
    previous_hbm,
    tables_hbm,
    out,
    potential_out,
    hopping,
    onsite,
    coupling,
    damping,
    occupation,
    tile_map,
    previous,
    tables,
    load,
    from_left,
    from_right,
    self_energy,
    relay,
    facts,
    columns,
    block,
    phonon,
    stencil,
    densities,
    weighted,
    landed,
    slab_send,
    slab_recv,
    energy_send,
    energy_recv,
    relay_recv,
    forward_send,
    fact_send,
    fact_recv,
    density_send,
    density_recv,
    plane_send,
    plane_recv,
):
    energies, slabs = axis_sizes
    e, s = lax.axis_index("energy"), lax.axis_index("slab")
    here = hopping.shape[-1]
    chunks = here // ROWS
    owned = 2
    half = energies // 2
    has = {
        "left": s > 0,
        "right": s < slabs - 1,
        "below": e > 0,
        "above": e < energies - 1,
    }
    device = {"left": (e, s - 1), "right": (e, s + 1), "below": (e - 1, s), "above": (e + 1, s)}
    crosses = {"above": e == half - 1, "below": e == half}

    def route(c):
        return jnp.where(lax.rem(c, 4) == 3, 2, lax.rem(c, 2))

    def relays(side, c):
        return (route(c) > 0) & (e == (energies - route(c) if side == "above" else route(c) - 1))


    barrier = pltpu.get_barrier_semaphore()
    for d in range(1, energies):
        pl.semaphore_signal(
            barrier, inc=1, device_id=(lax.rem(e + d, energies), s), device_id_type=MESH
        )
    for d in range(1, slabs):
        pl.semaphore_signal(
            barrier, inc=1, device_id=(e, lax.rem(s + d, slabs)), device_id_type=MESH
        )

    def loads():
        pairs = (
            (coupling_hbm, coupling),
            (damping_hbm, damping),
            (occupation_hbm, occupation),
            (onsite_hbm, onsite),
            (previous_hbm, previous),
            (tile_map_hbm, tile_map),
            (hopping_hbm, hopping),
            (tables_hbm.at[s], tables),
        )
        return [pltpu.make_async_copy(a, b, load.at[i]) for i, (a, b) in enumerate(pairs)]

    for copy in loads():
        copy.start()
    for copy in loads():
        copy.wait()

    facts[3, 0:1, :] = coupling[...]
    for k in range(owned):
        facts[3, 1 + k : 2 + k, :] = jnp.broadcast_to(damping[:, k : k + 1], (1, here))
        facts[3, 3 + k : 4 + k, :] = jnp.broadcast_to(occupation[:, k : k + 1], (1, here))

    pl.semaphore_wait(barrier, energies + slabs - 2)

    def slab_copy(side, c):
        k, row = c // chunks, pl.multiple_of(lax.rem(c, chunks) * ROWS, ROWS)
        index = 0 if side == "right" else 1
        landing = from_left if side == "right" else from_right
        return pltpu.make_async_remote_copy(
            src_ref=green.at[:, 0, k, pl.ds(row, ROWS), :],
            dst_ref=landing.at[c],
            send_sem=slab_send.at[index, c],
            recv_sem=slab_recv.at[index, c],
            device_id=device[side],
            device_id_type=MESH,
        )

    def energy_copy(side, c):
        k, row = c // chunks, pl.multiple_of(lax.rem(c, chunks) * ROWS, ROWS)
        index = 0 if side == "above" else 1
        return pltpu.make_async_remote_copy(
            src_ref=self_energy.at[0, k, :, pl.ds(row, ROWS), :],
            dst_ref=self_energy.at[1 + index, k, :, pl.ds(row, ROWS), :],
            send_sem=energy_send.at[index, c],
            recv_sem=energy_recv.at[index, c],
            device_id=device[side],
            device_id_type=MESH,
        )

    def relay_copy(side, c):
        k, row = c // chunks, pl.multiple_of(lax.rem(c, chunks) * ROWS, ROWS)
        index = 0 if side == "above" else 1
        return pltpu.make_async_remote_copy(
            src_ref=self_energy.at[0, k, :, pl.ds(row, ROWS), :],
            dst_ref=relay.at[c],
            send_sem=energy_send.at[index, c],
            recv_sem=relay_recv.at[c],
            device_id=(energies - route(c) if side == "above" else route(c) - 1, s),
            device_id_type=MESH,
        )

    def forward_copy(side, c):
        k, row = c // chunks, pl.multiple_of(lax.rem(c, chunks) * ROWS, ROWS)
        index = 0 if side == "above" else 1
        return pltpu.make_async_remote_copy(
            src_ref=relay.at[c],
            dst_ref=self_energy.at[1 + index, k, :, pl.ds(row, ROWS), :],
            send_sem=forward_send.at[c],
            recv_sem=energy_recv.at[index, c],
            device_id=(half if side == "above" else half - 1, s),
            device_id_type=MESH,
        )

    def forward(c):
        for side in ("above", "below"):

            @pl.when(relays(side, c))
            def _():
                relay_copy(side, c).wait_recv()
                forward_copy(side, c).start()

    def fact_copy(side):
        index = {"right": 0, "above": 1, "below": 2}[side]
        return pltpu.make_async_remote_copy(
            src_ref=facts.at[3],
            dst_ref=facts.at[index],
            send_sem=fact_send.at[index],
            recv_sem=fact_recv.at[index],
            device_id=device[side],
            device_id_type=MESH,
        )

    @pl.when(has["right"])
    def _():
        fact_copy("right").start()

    def send_green(c, carry):
        @pl.when(has["right"])
        def _():
            slab_copy("right", c).start()

        @pl.when(has["left"])
        def _():
            slab_copy("left", c).start()

        return carry

    lax.fori_loop(0, owned * chunks, send_green, 0)

    for side in ("above", "below"):

        @pl.when(has[side])
        def _():
            fact_copy(side).start()

    tall = potential_out.shape[1]
    width = potential_out.shape[2]

    def blocks(ref):
        own = ref[0, pl.ds(pl.multiple_of(e * tall, tall), tall), :]
        before = ref[0, pl.ds(pl.multiple_of(jnp.maximum(e - 1, 0) * tall, tall), tall), :]
        after = ref[
            0, pl.ds(pl.multiple_of(jnp.minimum(e + 1, energies - 1) * tall, tall), tall), :
        ]
        return before, own, after

    cell = lax.broadcasted_iota(jnp.int32, (3 * tall, width), 1)
    line = lax.broadcasted_iota(jnp.int32, (3 * tall, width), 0) + (e - 1) * tall
    inside = (line >= 0) & (line < energies * tall)

    def beside(field):
        up = pltpu.roll(field, 1, 0)
        down = pltpu.roll(field, 3 * tall - 1, 0)
        left = jnp.where(cell == 0, 0.0, pltpu.roll(field, 1, 1))
        right = jnp.where(cell == width - 1, 0.0, pltpu.roll(field, width - 1, 1))
        return up + down + left + right

    potential = jnp.where(inside, jnp.concatenate(blocks(previous), axis=0), 0.0)
    potential = jnp.where(inside, beside(potential), 0.0)
    stencil[...] = (ANISO * ANISO) * beside(potential)[tall : 2 * tall]

    rows = lax.broadcasted_iota(jnp.int32, (here, here), 0)
    lanes = lax.broadcasted_iota(jnp.int32, (here, here), 1)

    def column(row):
        return jnp.sum(jnp.where(rows == lanes, row, 0.0), axis=1, keepdims=True)

    columns[:, 0:1] = column(onsite[...])
    columns[:, 1:2] = column(coupling[...])

    @pl.when(jnp.logical_not(has["left"]))
    def _():
        from_left[...] = jnp.zeros_like(from_left)
        facts[0] = jnp.zeros_like(facts[0])

    @pl.when(jnp.logical_not(has["right"]))
    def _():
        from_right[...] = jnp.zeros_like(from_right)

    @pl.when(has["left"])
    def _():
        fact_copy("right").wait_recv()

    columns[:, 2:3] = column(facts[0, 0:1, :])

    def form_self_energy(c, carry):
        k, row = c // chunks, pl.multiple_of(lax.rem(c, chunks) * ROWS, ROWS)

        @pl.when(has["left"])
        def _():
            slab_copy("right", c).wait_recv()

        @pl.when(has["right"])
        def _():
            slab_copy("left", c).wait_recv()

        weight_left = columns[pl.ds(row, ROWS), 2:3] * facts[0, 0:1, :]
        weight_right = columns[pl.ds(row, ROWS), 1:2] * facts[3, 0:1, :]
        for part in range(2):
            self_energy[0, k, part, pl.ds(row, ROWS), :] = (
                weight_left * from_left[c, part] + weight_right * from_right[c, part]
            )
        for side in ("above", "below"):

            bent = crosses[side] & (route(c) > 0)

            @pl.when(has[side] & jnp.logical_not(bent))
            def _():
                energy_copy(side, c).start()

            @pl.when(bent)
            def _():
                relay_copy(side, c).start()

        @pl.when(c >= LAG)
        def _():
            forward(c - LAG)

        return carry

    def diagonal_inverse(energy, level, damp):
        real = energy - level
        modulus = real * real + damp * damp
        return real / modulus, -damp / modulus

    def step(t, carry):
        k, kind = t // 3, lax.rem(t, 3)
        lax.fori_loop(
            jnp.where(t == 0, 0, jnp.minimum(12 + 2 * t, owned * chunks)),
            jnp.minimum(14 + 2 * t, owned * chunks),
            form_self_energy,
            0,
        )

        @pl.when(t == 1)
        def _():
            for c in range(owned * chunks - LAG, owned * chunks):
                forward(c)

        side = jnp.where(lax.rem(e, half) >= half // 2, kind, 1 - kind)
        slot = jnp.where(kind == 2, 0, 1 + side)
        fact = jnp.where(kind == 2, 3, 1 + side)
        present = (kind == 2) | (jnp.where(side == 0, e, energies - 1 - e) > 0)

        def arrive(side):
            def one(c, inner):
                energy_copy(side, c).wait_recv()
                return inner

            lax.fori_loop(k * chunks, (k + 1) * chunks, one, 0)

            @pl.when(k == 0)
            def _():
                fact_copy(side).wait_recv()

        @pl.when((kind < 2) & (side == 0) & has["below"])
        def _():
            arrive("above")

        @pl.when((kind < 2) & (side == 1) & has["above"])
        def _():
            arrive("below")

        @pl.when(kind == 0)
        def _():
            phonon[...] = jnp.zeros_like(phonon)

        @pl.when(present)
        def _():
            place = owned * (e + jnp.where(kind == 2, 0, 2 * side - 1)) + k
            energy = -2.0 + 4.0 * (place.astype(F32) + 0.5) / (owned * energies)
            damp = facts[fact, pl.ds(1 + k, 1), :]
            x_real, x_imag = diagonal_inverse(energy, onsite[...], damp)
            se_real, se_imag = self_energy[slot, k, 0], self_energy[slot, k, 1]

            @pl.when(kind < 2)
            def _():
                block[0] = hopping[0] + se_real
                block[1] = se_imag

            @pl.when(kind == 2)
            def _():
                block[0] = hopping[0] + se_real + phonon[0]
                block[1] = se_imag + phonon[1]

            h_real, h_imag = block[0], block[1]
            a_real = h_real * x_real - h_imag * x_imag
            a_imag = h_real * x_imag + h_imag * x_real
            a = split(a_real, a_imag)
            square = product(a, a)
            two = split(*square)
            cube = product(a, two)
            fourth = product(two, two)
            t_real = a_real + square[0] + cube[0]
            t_imag = a_imag + square[1] + cube[1]
            rest = product(split(t_real, t_imag), split(*fourth))
            t_real = t_real + fourth[0] + rest[0]
            t_imag = t_imag + fourth[1] + rest[1]
            series = split(t_real, t_imag)

            fill = facts[fact, pl.ds(3 + k, 1), :]
            sigma_real = -fill * (se_real - se_real.T)
            sigma_imag = -fill * (se_imag + se_imag.T)

            @pl.when(kind < 2)
            def _():
                more = product(series, split(sigma_real, sigma_imag))
                w_real, w_imag = sigma_real + more[0], sigma_imag + more[1]
                adjoint = (series[0], halves(-t_imag), halves(t_real - t_imag))
                more = product(split(w_real, w_imag), adjoint, True)
                u_real, u_imag = w_real + more[0], w_imag + more[1]
                c_real, c_imag = diagonal_inverse(energy, columns[:, 0:1], damp[:, 0:1])
                c_real, c_imag = PHONON * c_real, PHONON * c_imag
                v_real = c_real * u_real - c_imag * u_imag
                v_imag = c_real * u_imag + c_imag * u_real
                unit = jnp.where(rows == lanes, 1.0, 0.0)
                g_real = unit + t_real
                phonon[0] += c_real * g_real - c_imag * t_imag
                phonon[1] += c_real * t_imag + c_imag * g_real
                phonon[2] += v_real * x_real + v_imag * x_imag
                phonon[3] += v_imag * x_real - v_real * x_imag

            @pl.when(kind == 2)
            def _():
                mixed_real = sigma_real + phonon[2]
                mixed_imag = sigma_imag + phonon[3]
                more = product(series, split(mixed_real, mixed_imag))
                w_real, w_imag = mixed_real + more[0], mixed_imag + more[1]
                terms = w_imag * t_real - w_real * t_imag + jnp.where(rows == lanes, w_imag, 0.0)
                total = jnp.sum(terms.T, axis=0, keepdims=True)
                out[pl.ds(k, 1), :] = (x_real * x_real + x_imag * x_imag) * total

        return carry

    lax.fori_loop(0, 3 * owned, step, 0)

    def settle(c, carry):
        for side in ("right", "left"):

            @pl.when(has[side])
            def _():
                slab_copy(side, c).wait_send()

        for side in ("above", "below"):

            @pl.when(has[side])
            def _():
                energy_copy(side, c).wait_send()

        @pl.when(relays("above", c) | relays("below", c))
        def _():
            forward_copy("above", c).wait_send()

        return carry

    def density_copy(d):
        return pltpu.make_async_remote_copy(
            src_ref=densities.at[e],
            dst_ref=densities.at[e],
            send_sem=density_send.at[d],
            recv_sem=density_recv.at[d],
            device_id=(lax.rem(e + d, energies), s),
            device_id_type=MESH,
        )

    def density_landing(d):
        slot = lax.rem(e + energies - d, energies)
        return pltpu.make_async_remote_copy(
            src_ref=densities.at[slot],
            dst_ref=densities.at[slot],
            send_sem=density_send.at[d],
            recv_sem=density_recv.at[d],
            device_id=(lax.rem(e + d, energies), s),
            device_id_type=MESH,
        )

    def plane_copy(d):
        return pltpu.make_async_remote_copy(
            src_ref=weighted.at[d],
            dst_ref=landed.at[d],
            send_sem=plane_send.at[d],
            recv_sem=plane_recv.at[d],
            device_id=(e, lax.rem(s + d, slabs)),
            device_id_type=MESH,
        )

    densities[e] = (4.0 / (owned * energies)) * jnp.sum(out[...], axis=0, keepdims=True)
    for d in range(1, energies):
        density_copy(d).start()
    for d in range(1, energies):
        density_landing(d).wait_recv()
    density = CHARGE * jnp.sum(densities[...], axis=0)

    index = jnp.concatenate(blocks(tile_map), axis=0)

    def spread(part):
        table = jnp.broadcast_to(density[:, part * width : (part + 1) * width], (3 * tall, width))
        return jnp.take_along_axis(table, index & (width - 1), axis=1)

    source = jnp.where(inside, jnp.where(index < width, spread(0), spread(1)), 0.0)
    second = ANISO * beside(source)[tall : 2 * tall] + stencil[...]
    source = source[tall : 2 * tall]
    for d in range(1, slabs):
        weighted[d] = tables[d, 0:1, :] * source + tables[d, 1:2, :] * second
        plane_copy(d).start()
    total = tables[0, 0:1, :] * source + tables[0, 1:2, :] * second
    for d in range(1, slabs):
        plane_copy(d).wait_recv()
        total = total + landed[d]
    potential_out[0] = total
    lax.fori_loop(0, owned * chunks, settle, 0)
    for side in ("right", "above", "below"):

        @pl.when(has[side])
        def _():
            fact_copy(side).wait_send()

    for d in range(1, energies):
        density_copy(d).wait_send()
    for d in range(1, slabs):
        plane_copy(d).wait_send()


def advance(axis_sizes, green, hopping, onsite, coupling, damping, occupation, tile_map, previous, tables):
    energies, slabs = axis_sizes
    size = hopping.shape[-1]
    count = 2 * (size // ROWS)
    tall, width = tile_map.shape[1] // energies, tile_map.shape[2]
    dma, vmem = pltpu.SemaphoreType.DMA, pl.BlockSpec(memory_space=pltpu.VMEM)
    local = (hopping, onsite, coupling, damping, occupation, tile_map, previous)
    return pl.pallas_call(
        functools.partial(step_kernel, axis_sizes),
        out_shape=(
            jax.ShapeDtypeStruct((2, size), F32),
            jax.ShapeDtypeStruct((1, tall, width), F32),
        ),
        in_specs=[pl.BlockSpec(memory_space=pl.ANY)] * 9,
        out_specs=(vmem, vmem),
        scratch_shapes=[
            *(pltpu.VMEM(array.shape, array.dtype) for array in local),
            pltpu.VMEM(tables.shape[1:], F32),
            dma((8,)),
            pltpu.VMEM((count, 2, ROWS, size), F32),
            pltpu.VMEM((count, 2, ROWS, size), F32),
            pltpu.VMEM((3, 2, 2, size, size), F32),
            pltpu.VMEM((count, 2, ROWS, size), F32),
            pltpu.VMEM((4, 8, size), F32),
            pltpu.VMEM((size, 128), F32),
            pltpu.VMEM((2, size, size), F32),
            pltpu.VMEM((4, size, size), F32),
            pltpu.VMEM((tall, width), F32),
            pltpu.VMEM((energies, 1, size), F32),
            pltpu.VMEM((slabs, tall, width), F32),
            pltpu.VMEM((slabs, tall, width), F32),
            dma((2, count)),
            dma((2, count)),
            dma((2, count)),
            dma((2, count)),
            dma((count,)),
            dma((count,)),
            dma((3,)),
            dma((3,)),
            dma((energies,)),
            dma((energies,)),
            dma((slabs,)),
            dma((slabs,)),
        ],
        compiler_params=pltpu.CompilerParams(
            collective_id=0, has_side_effects=True, vmem_limit_bytes=60 << 20
        ),
        name="step",
    )(green, hopping, onsite, coupling, damping, occupation, tile_map, previous, tables)


def solution(mesh):
    axis_sizes = (mesh.shape["energy"], mesh.shape["slab"])
    tables = line_tables(axis_sizes[1])

    def per_device(onsite, hopping, coupling, green, damping, occupation, tile_map, previous):
        lesser, potential = advance(
            axis_sizes,
            green,
            hopping,
            onsite,
            coupling,
            damping,
            occupation,
            tile_map,
            previous,
            jnp.asarray(tables),
        )

        def finish(a, b, c, d):
            c[0] = a[...]
            d[...] = b[...]

        return tuple(
            pl.pallas_call(
                finish,
                out_shape=(
                    jax.ShapeDtypeStruct((1, *lesser.shape), F32),
                    jax.ShapeDtypeStruct(potential.shape, F32),
                ),
                name="finish",
            )(lesser, potential)
        )

    in_specs = (
        P("slab", None),
        P("slab", None, None),
        P("slab", None),
        P(None, "slab", "energy", None, None),
        P("slab", "energy"),
        P("slab", "energy"),
        P("slab", None, None),
        P("slab", None, None),
    )
    out_specs = (P("slab", "energy", None), P("slab", "energy", None))
    return jax.shard_map(
        per_device, mesh=mesh, in_specs=in_specs, out_specs=out_specs, check_vma=False
    )
```

```python
import functools

import jax
import jax.numpy as jnp
import numpy as np
from jax import lax
from jax.experimental import pallas as pl
from jax.experimental.pallas import tpu as pltpu
from jax.sharding import PartitionSpec as P

F32 = jnp.float32
BF16 = jnp.bfloat16
MESH = pl.DeviceIdType.MESH
PHONON = 0.5
CHARGE = 2.0
ANISO = 0.05
SCREEN = 0.05
LAG = 3
WINDOW = 5
ROWS = 32


def line_tables(count):
    main = 2.0 + 4.0 * ANISO + SCREEN
    matrix = main * np.eye(count) - np.eye(count, k=1) - np.eye(count, k=-1)
    inverse = np.linalg.inv(matrix)
    around = (np.arange(count)[:, None] + np.arange(count)[None, :]) % count
    rows = np.arange(count)[:, None]
    weights = np.stack([inverse[rows, around], (inverse @ inverse)[rows, around]], axis=-1)
    return np.repeat(weights[..., None], 128, axis=-1).astype(np.float32)


def far_first(count):
    return sorted(range(1, count), key=lambda d: -min(d % (count // 2), -d % (count // 2)))


def middle_first(count):
    return sorted(range(1, count), key=lambda d: abs(d - count // 2))


def halves(value):
    high = value.astype(BF16)
    return high, (value - high.astype(F32)).astype(BF16)


def split(real, imag):
    return halves(real), halves(imag), halves(real + imag)


def times(first, second, turned):
    contract = (((1,), (1,)), ((), ())) if turned else (((1,), (0,)), ((), ()))

    def dot(a, b):
        return lax.dot_general(a, b, contract, preferred_element_type=F32)

    return dot(first[0], second[0]) + dot(first[0], second[1]) + dot(first[1], second[0])


def product(left, right, turned=False):
    one = times(left[0], right[0], turned)
    two = times(left[1], right[1], turned)
    both = times(left[2], right[2], turned)
    return one - two, both - one - two


def step_kernel(
    axis_sizes,
    green,
    hopping_hbm,
    onsite_hbm,
    coupling_hbm,
    damping_hbm,
    occupation_hbm,
    tile_map_hbm,
    previous_hbm,
    tables_hbm,
    out,
    potential_out,
    hopping,
    onsite,
    coupling,
    damping,
    occupation,
    tile_map,
    previous,
    tables,
    load,
    from_left,
    from_right,
    self_energy,
    relay,
    facts,
    columns,
    block,
    phonon,
    stencil,
    densities,
    weighted,
    landed,
    slab_send,
    slab_recv,
    energy_send,
    energy_recv,
    relay_recv,
    forward_send,
    fact_send,
    fact_recv,
    density_send,
    density_recv,
    plane_send,
    plane_recv,
):
    energies, slabs = axis_sizes
    e, s = lax.axis_index("energy"), lax.axis_index("slab")
    here = hopping.shape[-1]
    chunks = here // ROWS
    owned = 2
    half = energies // 2
    has = {
        "left": s > 0,
        "right": s < slabs - 1,
        "below": e > 0,
        "above": e < energies - 1,
    }
    device = {"left": (e, s - 1), "right": (e, s + 1), "below": (e - 1, s), "above": (e + 1, s)}
    crosses = {"above": e == half - 1, "below": e == half}

    def route(c):
        return jnp.where(lax.rem(c, 4) == 3, 2, lax.rem(c, 2))

    def relays(side, c):
        return (route(c) > 0) & (e == (energies - route(c) if side == "above" else route(c) - 1))


    barrier = pltpu.get_barrier_semaphore()
    for d in far_first(energies):
        pl.semaphore_signal(
            barrier, inc=1, device_id=(lax.rem(e + d, energies), s), device_id_type=MESH
        )
    for d in middle_first(slabs):
        pl.semaphore_signal(
            barrier, inc=1, device_id=(e, lax.rem(s + d, slabs)), device_id_type=MESH
        )

    def loads():
        pairs = (
            (coupling_hbm, coupling),
            (damping_hbm, damping),
            (occupation_hbm, occupation),
            (onsite_hbm, onsite),
            (previous_hbm, previous),
            (tile_map_hbm, tile_map),
            (hopping_hbm, hopping),
            (tables_hbm.at[s], tables),
        )
        return [pltpu.make_async_copy(a, b, load.at[i]) for i, (a, b) in enumerate(pairs)]

    for copy in loads():
        copy.start()
    for copy in loads():
        copy.wait()

    facts[3, 0:1, :] = coupling[...]
    for k in range(owned):
        facts[3, 1 + k : 2 + k, :] = jnp.broadcast_to(damping[:, k : k + 1], (1, here))
        facts[3, 3 + k : 4 + k, :] = jnp.broadcast_to(occupation[:, k : k + 1], (1, here))

    pl.semaphore_wait(barrier, energies + slabs - 2)

    def slab_copy(side, c):
        k, row = c // chunks, pl.multiple_of(lax.rem(c, chunks) * ROWS, ROWS)
        index = 0 if side == "right" else 1
        landing = from_left if side == "right" else from_right
        return pltpu.make_async_remote_copy(
            src_ref=green.at[:, 0, k, pl.ds(row, ROWS), :],
            dst_ref=landing.at[c],
            send_sem=slab_send.at[index, c],
            recv_sem=slab_recv.at[index, c],
            device_id=device[side],
            device_id_type=MESH,
        )

    def energy_copy(side, c):
        k, row = c // chunks, pl.multiple_of(lax.rem(c, chunks) * ROWS, ROWS)
        index = 0 if side == "above" else 1
        return pltpu.make_async_remote_copy(
            src_ref=self_energy.at[0, k, :, pl.ds(row, ROWS), :],
            dst_ref=self_energy.at[1 + index, k, :, pl.ds(row, ROWS), :],
            send_sem=energy_send.at[index, c],
            recv_sem=energy_recv.at[index, c],
            device_id=device[side],
            device_id_type=MESH,
        )

    def relay_copy(side, c):
        k, row = c // chunks, pl.multiple_of(lax.rem(c, chunks) * ROWS, ROWS)
        index = 0 if side == "above" else 1
        return pltpu.make_async_remote_copy(
            src_ref=self_energy.at[0, k, :, pl.ds(row, ROWS), :],
            dst_ref=relay.at[c],
            send_sem=energy_send.at[index, c],
            recv_sem=relay_recv.at[c],
            device_id=(energies - route(c) if side == "above" else route(c) - 1, s),
            device_id_type=MESH,
        )

    def forward_copy(side, c):
        k, row = c // chunks, pl.multiple_of(lax.rem(c, chunks) * ROWS, ROWS)
        index = 0 if side == "above" else 1
        return pltpu.make_async_remote_copy(
            src_ref=relay.at[c],
            dst_ref=self_energy.at[1 + index, k, :, pl.ds(row, ROWS), :],
            send_sem=forward_send.at[c],
            recv_sem=energy_recv.at[index, c],
            device_id=(half if side == "above" else half - 1, s),
            device_id_type=MESH,
        )

    def forward(c):
        for side in ("above", "below"):

            @pl.when(relays(side, c))
            def _():
                relay_copy(side, c).wait_recv()
                forward_copy(side, c).start()

    def fact_copy(side):
        index = {"right": 0, "above": 1, "below": 2}[side]
        return pltpu.make_async_remote_copy(
            src_ref=facts.at[3],
            dst_ref=facts.at[index],
            send_sem=fact_send.at[index],
            recv_sem=fact_recv.at[index],
            device_id=device[side],
            device_id_type=MESH,
        )

    @pl.when(has["right"])
    def _():
        fact_copy("right").start()

    def send_green(c, carry):
        @pl.when(has["right"])
        def _():
            slab_copy("right", c).start()

        @pl.when(has["left"])
        def _():
            slab_copy("left", c).start()

        return carry

    lax.fori_loop(0, WINDOW, send_green, 0)

    for side in ("above", "below"):

        @pl.when(has[side])
        def _():
            fact_copy(side).start()

    tall = potential_out.shape[1]
    width = potential_out.shape[2]

    def blocks(ref):
        own = ref[0, pl.ds(pl.multiple_of(e * tall, tall), tall), :]
        before = ref[0, pl.ds(pl.multiple_of(jnp.maximum(e - 1, 0) * tall, tall), tall), :]
        after = ref[
            0, pl.ds(pl.multiple_of(jnp.minimum(e + 1, energies - 1) * tall, tall), tall), :
        ]
        return before, own, after

    cell = lax.broadcasted_iota(jnp.int32, (3 * tall, width), 1)
    line = lax.broadcasted_iota(jnp.int32, (3 * tall, width), 0) + (e - 1) * tall
    inside = (line >= 0) & (line < energies * tall)

    def beside(field):
        up = pltpu.roll(field, 1, 0)
        down = pltpu.roll(field, 3 * tall - 1, 0)
        left = jnp.where(cell == 0, 0.0, pltpu.roll(field, 1, 1))
        right = jnp.where(cell == width - 1, 0.0, pltpu.roll(field, width - 1, 1))
        return up + down + left + right

    potential = jnp.where(inside, jnp.concatenate(blocks(previous), axis=0), 0.0)
    potential = jnp.where(inside, beside(potential), 0.0)
    stencil[...] = (ANISO * ANISO) * beside(potential)[tall : 2 * tall]

    rows = lax.broadcasted_iota(jnp.int32, (here, here), 0)
    lanes = lax.broadcasted_iota(jnp.int32, (here, here), 1)

    def column(row):
        return jnp.sum(jnp.where(rows == lanes, row, 0.0), axis=1, keepdims=True)

    columns[:, 0:1] = column(onsite[...])
    columns[:, 1:2] = column(coupling[...])

    @pl.when(jnp.logical_not(has["left"]))
    def _():
        from_left[...] = jnp.zeros_like(from_left)
        facts[0] = jnp.zeros_like(facts[0])

    @pl.when(jnp.logical_not(has["right"]))
    def _():
        from_right[...] = jnp.zeros_like(from_right)

    @pl.when(has["left"])
    def _():
        fact_copy("right").wait_recv()

    columns[:, 2:3] = column(facts[0, 0:1, :])

    def form_self_energy(c, carry):
        k, row = c // chunks, pl.multiple_of(lax.rem(c, chunks) * ROWS, ROWS)

        @pl.when(has["left"])
        def _():
            slab_copy("right", c).wait_recv()

        @pl.when(has["right"])
        def _():
            slab_copy("left", c).wait_recv()

        @pl.when(c + WINDOW < owned * chunks)
        def _():
            send_green(c + WINDOW, 0)

        weight_left = columns[pl.ds(row, ROWS), 2:3] * facts[0, 0:1, :]
        weight_right = columns[pl.ds(row, ROWS), 1:2] * facts[3, 0:1, :]
        for part in range(2):
            self_energy[0, k, part, pl.ds(row, ROWS), :] = (
                weight_left * from_left[c, part] + weight_right * from_right[c, part]
            )
        for side in ("above", "below"):

            bent = crosses[side] & (route(c) > 0)

            @pl.when(has[side] & jnp.logical_not(bent))
            def _():
                energy_copy(side, c).start()

            @pl.when(bent)
            def _():
                relay_copy(side, c).start()

        @pl.when(c >= LAG)
        def _():
            forward(c - LAG)

        return carry

    def diagonal_inverse(energy, level, damp):
        real = energy - level
        modulus = real * real + damp * damp
        return real / modulus, -damp / modulus

    def step(t, carry):
        k, kind = t // 3, lax.rem(t, 3)
        lax.fori_loop(
            jnp.where(t == 0, 0, jnp.minimum(12 + 2 * t, owned * chunks)),
            jnp.minimum(14 + 2 * t, owned * chunks),
            form_self_energy,
            0,
        )

        @pl.when(t == 2)
        def _():
            forward(owned * chunks - 3)
            forward(owned * chunks - 2)
            forward(owned * chunks - 1)

        side = jnp.where(lax.rem(e, half) >= half // 2, kind, 1 - kind)
        slot = jnp.where(kind == 2, 0, 1 + side)
        fact = jnp.where(kind == 2, 3, 1 + side)
        present = (kind == 2) | (jnp.where(side == 0, e, energies - 1 - e) > 0)

        def arrive(side):
            def one(c, inner):
                energy_copy(side, c).wait_recv()
                return inner

            lax.fori_loop(k * chunks, (k + 1) * chunks, one, 0)

            @pl.when(k == 0)
            def _():
                fact_copy(side).wait_recv()

        @pl.when((kind < 2) & (side == 0) & has["below"])
        def _():
            arrive("above")

        @pl.when((kind < 2) & (side == 1) & has["above"])
        def _():
            arrive("below")

        @pl.when(kind == 0)
        def _():
            phonon[...] = jnp.zeros_like(phonon)

        @pl.when(present)
        def _():
            place = owned * (e + jnp.where(kind == 2, 0, 2 * side - 1)) + k
            energy = -2.0 + 4.0 * (place.astype(F32) + 0.5) / (owned * energies)
            damp = facts[fact, pl.ds(1 + k, 1), :]
            x_real, x_imag = diagonal_inverse(energy, onsite[...], damp)
            se_real, se_imag = self_energy[slot, k, 0], self_energy[slot, k, 1]

            @pl.when(kind < 2)
            def _():
                block[0] = hopping[0] + se_real
                block[1] = se_imag

            @pl.when(kind == 2)
            def _():
                block[0] = hopping[0] + se_real + phonon[0]
                block[1] = se_imag + phonon[1]

            h_real, h_imag = block[0], block[1]
            a_real = h_real * x_real - h_imag * x_imag
            a_imag = h_real * x_imag + h_imag * x_real
            a = split(a_real, a_imag)
            square = product(a, a)
            two = split(*square)
            cube = product(a, two)
            fourth = product(two, two)
            t_real = a_real + square[0] + cube[0]
            t_imag = a_imag + square[1] + cube[1]
            rest = product(split(t_real, t_imag), split(*fourth))
            t_real = t_real + fourth[0] + rest[0]
            t_imag = t_imag + fourth[1] + rest[1]
            series = split(t_real, t_imag)

            fill = facts[fact, pl.ds(3 + k, 1), :]
            sigma_real = -fill * (se_real - se_real.T)
            sigma_imag = -fill * (se_imag + se_imag.T)

            @pl.when(kind < 2)
            def _():
                more = product(series, split(sigma_real, sigma_imag))
                w_real, w_imag = sigma_real + more[0], sigma_imag + more[1]
                adjoint = (series[0], halves(-t_imag), halves(t_real - t_imag))
                more = product(split(w_real, w_imag), adjoint, True)
                u_real, u_imag = w_real + more[0], w_imag + more[1]
                c_real, c_imag = diagonal_inverse(energy, columns[:, 0:1], damp[:, 0:1])
                c_real, c_imag = PHONON * c_real, PHONON * c_imag
                v_real = c_real * u_real - c_imag * u_imag
                v_imag = c_real * u_imag + c_imag * u_real
                unit = jnp.where(rows == lanes, 1.0, 0.0)
                g_real = unit + t_real
                phonon[0] += c_real * g_real - c_imag * t_imag
                phonon[1] += c_real * t_imag + c_imag * g_real
                phonon[2] += v_real * x_real + v_imag * x_imag
                phonon[3] += v_imag * x_real - v_real * x_imag

            @pl.when(kind == 2)
            def _():
                mixed_real = sigma_real + phonon[2]
                mixed_imag = sigma_imag + phonon[3]
                more = product(series, split(mixed_real, mixed_imag))
                w_real, w_imag = mixed_real + more[0], mixed_imag + more[1]
                terms = w_imag * t_real - w_real * t_imag + jnp.where(rows == lanes, w_imag, 0.0)
                total = jnp.sum(terms.T, axis=0, keepdims=True)
                out[pl.ds(k, 1), :] = (x_real * x_real + x_imag * x_imag) * total

        return carry

    lax.fori_loop(0, 3 * owned, step, 0)

    def settle(c, carry):
        for side in ("right", "left"):

            @pl.when(has[side])
            def _():
                slab_copy(side, c).wait_send()

        for side in ("above", "below"):

            @pl.when(has[side])
            def _():
                energy_copy(side, c).wait_send()

        @pl.when(relays("above", c) | relays("below", c))
        def _():
            forward_copy("above", c).wait_send()

        return carry

    def density_copy(d):
        return pltpu.make_async_remote_copy(
            src_ref=densities.at[e],
            dst_ref=densities.at[e],
            send_sem=density_send.at[d],
            recv_sem=density_recv.at[d],
            device_id=(lax.rem(e + d, energies), s),
            device_id_type=MESH,
        )

    def density_landing(d):
        slot = lax.rem(e + energies - d, energies)
        return pltpu.make_async_remote_copy(
            src_ref=densities.at[slot],
            dst_ref=densities.at[slot],
            send_sem=density_send.at[d],
            recv_sem=density_recv.at[d],
            device_id=(lax.rem(e + d, energies), s),
            device_id_type=MESH,
        )

    def plane_copy(d):
        return pltpu.make_async_remote_copy(
            src_ref=weighted.at[d],
            dst_ref=landed.at[d],
            send_sem=plane_send.at[d],
            recv_sem=plane_recv.at[d],
            device_id=(e, lax.rem(s + d, slabs)),
            device_id_type=MESH,
        )

    densities[e] = (4.0 / (owned * energies)) * jnp.sum(out[...], axis=0, keepdims=True)
    for d in far_first(energies):
        density_copy(d).start()
    for d in range(1, energies):
        density_landing(d).wait_recv()
    density = CHARGE * jnp.sum(densities[...], axis=0)

    index = jnp.concatenate(blocks(tile_map), axis=0)

    def spread(part):
        table = jnp.broadcast_to(density[:, part * width : (part + 1) * width], (3 * tall, width))
        return jnp.take_along_axis(table, index & (width - 1), axis=1)

    source = jnp.where(inside, jnp.where(index < width, spread(0), spread(1)), 0.0)
    second = ANISO * beside(source)[tall : 2 * tall] + stencil[...]
    source = source[tall : 2 * tall]
    for d in middle_first(slabs):
        weighted[d] = tables[d, 0:1, :] * source + tables[d, 1:2, :] * second
        plane_copy(d).start()
    total = tables[0, 0:1, :] * source + tables[0, 1:2, :] * second
    for d in range(1, slabs):
        plane_copy(d).wait_recv()
        total = total + landed[d]
    potential_out[0] = total
    lax.fori_loop(0, owned * chunks, settle, 0)
    for side in ("right", "above", "below"):

        @pl.when(has[side])
        def _():
            fact_copy(side).wait_send()

    for d in range(1, energies):
        density_copy(d).wait_send()
    for d in range(1, slabs):
        plane_copy(d).wait_send()


def advance(axis_sizes, green, hopping, onsite, coupling, damping, occupation, tile_map, previous, tables):
    energies, slabs = axis_sizes
    size = hopping.shape[-1]
    count = 2 * (size // ROWS)
    tall, width = tile_map.shape[1] // energies, tile_map.shape[2]
    dma, vmem = pltpu.SemaphoreType.DMA, pl.BlockSpec(memory_space=pltpu.VMEM)
    local = (hopping, onsite, coupling, damping, occupation, tile_map, previous)
    return pl.pallas_call(
        functools.partial(step_kernel, axis_sizes),
        out_shape=(
            jax.ShapeDtypeStruct((2, size), F32),
            jax.ShapeDtypeStruct((1, tall, width), F32),
        ),
        in_specs=[pl.BlockSpec(memory_space=pl.ANY)] * 9,
        out_specs=(vmem, vmem),
        scratch_shapes=[
            *(pltpu.VMEM(array.shape, array.dtype) for array in local),
            pltpu.VMEM(tables.shape[1:], F32),
            dma((8,)),
            pltpu.VMEM((count, 2, ROWS, size), F32),
            pltpu.VMEM((count, 2, ROWS, size), F32),
            pltpu.VMEM((3, 2, 2, size, size), F32),
            pltpu.VMEM((count, 2, ROWS, size), F32),
            pltpu.VMEM((4, 8, size), F32),
            pltpu.VMEM((size, 128), F32),
            pltpu.VMEM((2, size, size), F32),
            pltpu.VMEM((4, size, size), F32),
            pltpu.VMEM((tall, width), F32),
            pltpu.VMEM((energies, 1, size), F32),
            pltpu.VMEM((slabs, tall, width), F32),
            pltpu.VMEM((slabs, tall, width), F32),
            dma((2, count)),
            dma((2, count)),
            dma((2, count)),
            dma((2, count)),
            dma((count,)),
            dma((count,)),
            dma((3,)),
            dma((3,)),
            dma((energies,)),
            dma((energies,)),
            dma((slabs,)),
            dma((slabs,)),
        ],
        compiler_params=pltpu.CompilerParams(
            collective_id=0, has_side_effects=True, vmem_limit_bytes=60 << 20
        ),
        name="step",
    )(green, hopping, onsite, coupling, damping, occupation, tile_map, previous, tables)


def solution(mesh):
    axis_sizes = (mesh.shape["energy"], mesh.shape["slab"])
    tables = line_tables(axis_sizes[1])

    def per_device(onsite, hopping, coupling, green, damping, occupation, tile_map, previous):
        lesser, potential = advance(
            axis_sizes,
            green,
            hopping,
            onsite,
            coupling,
            damping,
            occupation,
            tile_map,
            previous,
            jnp.asarray(tables),
        )

        def finish(a, b, c, d):
            c[0] = a[...]
            d[...] = b[...]

        return tuple(
            pl.pallas_call(
                finish,
                out_shape=(
                    jax.ShapeDtypeStruct((1, *lesser.shape), F32),
                    jax.ShapeDtypeStruct(potential.shape, F32),
                ),
                name="finish",
            )(lesser, potential)
        )

    in_specs = (
        P("slab", None),
        P("slab", None, None),
        P("slab", None),
        P(None, "slab", "energy", None, None),
        P("slab", "energy"),
        P("slab", "energy"),
        P("slab", None, None),
        P("slab", None, None),
    )
    out_specs = (P("slab", "energy", None), P("slab", "energy", None))
    return jax.shard_map(
        per_device, mesh=mesh, in_specs=in_specs, out_specs=out_specs, check_vma=False
    )
```

```python
import functools

import jax
import jax.numpy as jnp
import numpy as np
from jax import lax
from jax.experimental import pallas as pl
from jax.experimental.pallas import tpu as pltpu
from jax.sharding import PartitionSpec as P

F32 = jnp.float32
BF16 = jnp.bfloat16
MESH = pl.DeviceIdType.MESH
PHONON = 0.5
CHARGE = 2.0
ANISO = 0.05
SCREEN = 0.05
LAG = 3
WINDOW = 5
ROWS = 32


def line_tables(count):
    main = 2.0 + 4.0 * ANISO + SCREEN
    matrix = main * np.eye(count) - np.eye(count, k=1) - np.eye(count, k=-1)
    inverse = np.linalg.inv(matrix)
    around = (np.arange(count)[:, None] + np.arange(count)[None, :]) % count
    rows = np.arange(count)[:, None]
    weights = np.stack([inverse[rows, around], (inverse @ inverse)[rows, around]], axis=-1)
    return np.repeat(weights[..., None], 128, axis=-1).astype(np.float32)


def far_first(count):
    return sorted(range(1, count), key=lambda d: -min(d % (count // 2), -d % (count // 2)))


def middle_first(count):
    return sorted(range(1, count), key=lambda d: abs(d - count // 2))


def halves(value):
    high = value.astype(BF16)
    return high, (value - high.astype(F32)).astype(BF16)


def split(real, imag):
    return halves(real), halves(imag), halves(real + imag)


def times(first, second, turned):
    contract = (((1,), (1,)), ((), ())) if turned else (((1,), (0,)), ((), ()))

    def dot(a, b):
        return lax.dot_general(a, b, contract, preferred_element_type=F32)

    return dot(first[0], second[0]) + dot(first[0], second[1]) + dot(first[1], second[0])


def product(left, right, turned=False):
    one = times(left[0], right[0], turned)
    two = times(left[1], right[1], turned)
    both = times(left[2], right[2], turned)
    return one - two, both - one - two


def step_kernel(
    axis_sizes,
    green,
    hopping_hbm,
    onsite_hbm,
    coupling_hbm,
    damping_hbm,
    occupation_hbm,
    tile_map_hbm,
    previous_hbm,
    tables_hbm,
    out,
    potential_out,
    hopping,
    onsite,
    coupling,
    damping,
    occupation,
    tile_map,
    previous,
    tables,
    load,
    from_left,
    from_right,
    self_energy,
    relay,
    facts,
    columns,
    block,
    phonon,
    stencil,
    densities,
    weighted,
    landed,
    slab_send,
    slab_recv,
    energy_send,
    energy_recv,
    relay_recv,
    forward_send,
    fact_send,
    fact_recv,
    density_send,
    density_recv,
    plane_send,
    plane_recv,
):
    energies, slabs = axis_sizes
    e, s = lax.axis_index("energy"), lax.axis_index("slab")
    here = hopping.shape[-1]
    chunks = here // ROWS
    owned = 2
    half = energies // 2
    has = {
        "left": s > 0,
        "right": s < slabs - 1,
        "below": e > 0,
        "above": e < energies - 1,
    }
    device = {"left": (e, s - 1), "right": (e, s + 1), "below": (e - 1, s), "above": (e + 1, s)}
    crosses = {"above": e == half - 1, "below": e == half}

    def route(c):
        return lax.rem(c, 3)

    def relays(side, c):
        return (route(c) > 0) & (e == (energies - route(c) if side == "above" else route(c) - 1))


    barrier = pltpu.get_barrier_semaphore()
    for d in far_first(energies):
        pl.semaphore_signal(
            barrier, inc=1, device_id=(lax.rem(e + d, energies), s), device_id_type=MESH
        )
    for d in middle_first(slabs):
        pl.semaphore_signal(
            barrier, inc=1, device_id=(e, lax.rem(s + d, slabs)), device_id_type=MESH
        )

    def loads():
        pairs = (
            (coupling_hbm, coupling),
            (damping_hbm, damping),
            (occupation_hbm, occupation),
            (onsite_hbm, onsite),
            (previous_hbm, previous),
            (tile_map_hbm, tile_map),
            (hopping_hbm, hopping),
            (tables_hbm.at[s], tables),
        )
        return [pltpu.make_async_copy(a, b, load.at[i]) for i, (a, b) in enumerate(pairs)]

    for copy in loads():
        copy.start()
    for copy in loads():
        copy.wait()

    facts[3, 0:1, :] = coupling[...]
    for k in range(owned):
        facts[3, 1 + k : 2 + k, :] = jnp.broadcast_to(damping[:, k : k + 1], (1, here))
        facts[3, 3 + k : 4 + k, :] = jnp.broadcast_to(occupation[:, k : k + 1], (1, here))

    pl.semaphore_wait(barrier, energies + slabs - 2)

    def slab_copy(side, c):
        k, row = c // chunks, pl.multiple_of(lax.rem(c, chunks) * ROWS, ROWS)
        index = 0 if side == "right" else 1
        landing = from_left if side == "right" else from_right
        return pltpu.make_async_remote_copy(
            src_ref=green.at[:, 0, k, pl.ds(row, ROWS), :],
            dst_ref=landing.at[c],
            send_sem=slab_send.at[index, c],
            recv_sem=slab_recv.at[index, c],
            device_id=device[side],
            device_id_type=MESH,
        )

    def energy_copy(side, c):
        k, row = c // chunks, pl.multiple_of(lax.rem(c, chunks) * ROWS, ROWS)
        index = 0 if side == "above" else 1
        return pltpu.make_async_remote_copy(
            src_ref=self_energy.at[0, k, :, pl.ds(row, ROWS), :],
            dst_ref=self_energy.at[1 + index, k, :, pl.ds(row, ROWS), :],
            send_sem=energy_send.at[index, c],
            recv_sem=energy_recv.at[index, c],
            device_id=device[side],
            device_id_type=MESH,
        )

    def relay_copy(side, c):
        k, row = c // chunks, pl.multiple_of(lax.rem(c, chunks) * ROWS, ROWS)
        index = 0 if side == "above" else 1
        return pltpu.make_async_remote_copy(
            src_ref=self_energy.at[0, k, :, pl.ds(row, ROWS), :],
            dst_ref=relay.at[c],
            send_sem=energy_send.at[index, c],
            recv_sem=relay_recv.at[c],
            device_id=(energies - route(c) if side == "above" else route(c) - 1, s),
            device_id_type=MESH,
        )

    def forward_copy(side, c):
        k, row = c // chunks, pl.multiple_of(lax.rem(c, chunks) * ROWS, ROWS)
        index = 0 if side == "above" else 1
        return pltpu.make_async_remote_copy(
            src_ref=relay.at[c],
            dst_ref=self_energy.at[1 + index, k, :, pl.ds(row, ROWS), :],
            send_sem=forward_send.at[c],
            recv_sem=energy_recv.at[index, c],
            device_id=(half if side == "above" else half - 1, s),
            device_id_type=MESH,
        )

    def forward(c):
        for side in ("above", "below"):

            @pl.when(relays(side, c))
            def _():
                relay_copy(side, c).wait_recv()
                forward_copy(side, c).start()

    def fact_copy(side):
        index = {"right": 0, "above": 1, "below": 2}[side]
        return pltpu.make_async_remote_copy(
            src_ref=facts.at[3],
            dst_ref=facts.at[index],
            send_sem=fact_send.at[index],
            recv_sem=fact_recv.at[index],
            device_id=device[side],
            device_id_type=MESH,
        )

    @pl.when(has["right"])
    def _():
        fact_copy("right").start()

    def send_green(c, carry):
        @pl.when(has["right"])
        def _():
            slab_copy("right", c).start()

        @pl.when(has["left"])
        def _():
            slab_copy("left", c).start()

        return carry

    lax.fori_loop(0, WINDOW, send_green, 0)

    for side in ("above", "below"):

        @pl.when(has[side])
        def _():
            fact_copy(side).start()

    tall = potential_out.shape[1]
    width = potential_out.shape[2]

    def blocks(ref):
        own = ref[0, pl.ds(pl.multiple_of(e * tall, tall), tall), :]
        before = ref[0, pl.ds(pl.multiple_of(jnp.maximum(e - 1, 0) * tall, tall), tall), :]
        after = ref[
            0, pl.ds(pl.multiple_of(jnp.minimum(e + 1, energies - 1) * tall, tall), tall), :
        ]
        return before, own, after

    cell = lax.broadcasted_iota(jnp.int32, (3 * tall, width), 1)
    line = lax.broadcasted_iota(jnp.int32, (3 * tall, width), 0) + (e - 1) * tall
    inside = (line >= 0) & (line < energies * tall)

    def beside(field):
        up = pltpu.roll(field, 1, 0)
        down = pltpu.roll(field, 3 * tall - 1, 0)
        left = jnp.where(cell == 0, 0.0, pltpu.roll(field, 1, 1))
        right = jnp.where(cell == width - 1, 0.0, pltpu.roll(field, width - 1, 1))
        return up + down + left + right

    potential = jnp.where(inside, jnp.concatenate(blocks(previous), axis=0), 0.0)
    potential = jnp.where(inside, beside(potential), 0.0)
    stencil[...] = (ANISO * ANISO) * beside(potential)[tall : 2 * tall]

    rows = lax.broadcasted_iota(jnp.int32, (here, here), 0)
    lanes = lax.broadcasted_iota(jnp.int32, (here, here), 1)

    def column(row):
        return jnp.sum(jnp.where(rows == lanes, row, 0.0), axis=1, keepdims=True)

    columns[:, 0:1] = column(onsite[...])
    columns[:, 1:2] = column(coupling[...])

    @pl.when(jnp.logical_not(has["left"]))
    def _():
        from_left[...] = jnp.zeros_like(from_left)
        facts[0] = jnp.zeros_like(facts[0])

    @pl.when(jnp.logical_not(has["right"]))
    def _():
        from_right[...] = jnp.zeros_like(from_right)

    @pl.when(has["left"])
    def _():
        fact_copy("right").wait_recv()

    columns[:, 2:3] = column(facts[0, 0:1, :])

    def form_self_energy(c, carry):
        k, row = c // chunks, pl.multiple_of(lax.rem(c, chunks) * ROWS, ROWS)

        @pl.when(has["left"])
        def _():
            slab_copy("right", c).wait_recv()

        @pl.when(has["right"])
        def _():
            slab_copy("left", c).wait_recv()

        @pl.when(c + WINDOW < owned * chunks)
        def _():
            send_green(c + WINDOW, 0)

        weight_left = columns[pl.ds(row, ROWS), 2:3] * facts[0, 0:1, :]
        weight_right = columns[pl.ds(row, ROWS), 1:2] * facts[3, 0:1, :]
        for part in range(2):
            self_energy[0, k, part, pl.ds(row, ROWS), :] = (
                weight_left * from_left[c, part] + weight_right * from_right[c, part]
            )
        for side in ("above", "below"):

            bent = crosses[side] & (route(c) > 0)

            @pl.when(has[side] & jnp.logical_not(bent))
            def _():
                energy_copy(side, c).start()

            @pl.when(bent)
            def _():
                relay_copy(side, c).start()

        @pl.when(c >= LAG)
        def _():
            forward(c - LAG)

        return carry

    def diagonal_inverse(energy, level, damp):
        real = energy - level
        modulus = real * real + damp * damp
        return real / modulus, -damp / modulus

    def step(t, carry):
        k, kind = t // 3, lax.rem(t, 3)
        lax.fori_loop(
            jnp.where(t == 0, 0, jnp.minimum(12 + 2 * t, owned * chunks)),
            jnp.minimum(14 + 2 * t, owned * chunks),
            form_self_energy,
            0,
        )

        @pl.when(t == 2)
        def _():
            forward(owned * chunks - 3)
            forward(owned * chunks - 2)
            forward(owned * chunks - 1)

        side = jnp.where(lax.rem(e, half) >= half // 2, kind, 1 - kind)
        slot = jnp.where(kind == 2, 0, 1 + side)
        fact = jnp.where(kind == 2, 3, 1 + side)
        present = (kind == 2) | (jnp.where(side == 0, e, energies - 1 - e) > 0)

        def arrive(side):
            def one(c, inner):
                energy_copy(side, c).wait_recv()
                return inner

            lax.fori_loop(k * chunks, (k + 1) * chunks, one, 0)

            @pl.when(k == 0)
            def _():
                fact_copy(side).wait_recv()

        @pl.when((kind < 2) & (side == 0) & has["below"])
        def _():
            arrive("above")

        @pl.when((kind < 2) & (side == 1) & has["above"])
        def _():
            arrive("below")

        @pl.when(kind == 0)
        def _():
            phonon[...] = jnp.zeros_like(phonon)

        @pl.when(present)
        def _():
            place = owned * (e + jnp.where(kind == 2, 0, 2 * side - 1)) + k
            energy = -2.0 + 4.0 * (place.astype(F32) + 0.5) / (owned * energies)
            damp = facts[fact, pl.ds(1 + k, 1), :]
            x_real, x_imag = diagonal_inverse(energy, onsite[...], damp)
            se_real, se_imag = self_energy[slot, k, 0], self_energy[slot, k, 1]

            @pl.when(kind < 2)
            def _():
                block[0] = hopping[0] + se_real
                block[1] = se_imag

            @pl.when(kind == 2)
            def _():
                block[0] = hopping[0] + se_real + phonon[0]
                block[1] = se_imag + phonon[1]

            h_real, h_imag = block[0], block[1]
            a_real = h_real * x_real - h_imag * x_imag
            a_imag = h_real * x_imag + h_imag * x_real
            a = split(a_real, a_imag)
            square = product(a, a)
            two = split(*square)
            cube = product(a, two)
            fourth = product(two, two)
            t_real = a_real + square[0] + cube[0]
            t_imag = a_imag + square[1] + cube[1]
            rest = product(split(t_real, t_imag), split(*fourth))
            t_real = t_real + fourth[0] + rest[0]
            t_imag = t_imag + fourth[1] + rest[1]
            series = split(t_real, t_imag)

            fill = facts[fact, pl.ds(3 + k, 1), :]
            sigma_real = -fill * (se_real - se_real.T)
            sigma_imag = -fill * (se_imag + se_imag.T)

            @pl.when(kind < 2)
            def _():
                more = product(series, split(sigma_real, sigma_imag))
                w_real, w_imag = sigma_real + more[0], sigma_imag + more[1]
                adjoint = (series[0], halves(-t_imag), halves(t_real - t_imag))
                more = product(split(w_real, w_imag), adjoint, True)
                u_real, u_imag = w_real + more[0], w_imag + more[1]
                c_real, c_imag = diagonal_inverse(energy, columns[:, 0:1], damp[:, 0:1])
                c_real, c_imag = PHONON * c_real, PHONON * c_imag
                v_real = c_real * u_real - c_imag * u_imag
                v_imag = c_real * u_imag + c_imag * u_real
                unit = jnp.where(rows == lanes, 1.0, 0.0)
                g_real = unit + t_real
                phonon[0] += c_real * g_real - c_imag * t_imag
                phonon[1] += c_real * t_imag + c_imag * g_real
                phonon[2] += v_real * x_real + v_imag * x_imag
                phonon[3] += v_imag * x_real - v_real * x_imag

            @pl.when(kind == 2)
            def _():
                mixed_real = sigma_real + phonon[2]
                mixed_imag = sigma_imag + phonon[3]
                more = product(series, split(mixed_real, mixed_imag))
                w_real, w_imag = mixed_real + more[0], mixed_imag + more[1]
                terms = w_imag * t_real - w_real * t_imag + jnp.where(rows == lanes, w_imag, 0.0)
                total = jnp.sum(terms.T, axis=0, keepdims=True)
                out[pl.ds(k, 1), :] = (x_real * x_real + x_imag * x_imag) * total

        return carry

    lax.fori_loop(0, 3 * owned, step, 0)

    def settle(c, carry):
        for side in ("right", "left"):

            @pl.when(has[side])
            def _():
                slab_copy(side, c).wait_send()

        for side in ("above", "below"):

            @pl.when(has[side])
            def _():
                energy_copy(side, c).wait_send()

        @pl.when(relays("above", c) | relays("below", c))
        def _():
            forward_copy("above", c).wait_send()

        return carry

    def density_copy(d):
        return pltpu.make_async_remote_copy(
            src_ref=densities.at[e],
            dst_ref=densities.at[e],
            send_sem=density_send.at[d],
            recv_sem=density_recv.at[d],
            device_id=(lax.rem(e + d, energies), s),
            device_id_type=MESH,
        )

    def density_landing(d):
        slot = lax.rem(e + energies - d, energies)
        return pltpu.make_async_remote_copy(
            src_ref=densities.at[slot],
            dst_ref=densities.at[slot],
            send_sem=density_send.at[d],
            recv_sem=density_recv.at[d],
            device_id=(lax.rem(e + d, energies), s),
            device_id_type=MESH,
        )

    def plane_copy(d):
        return pltpu.make_async_remote_copy(
            src_ref=weighted.at[d],
            dst_ref=landed.at[d],
            send_sem=plane_send.at[d],
            recv_sem=plane_recv.at[d],
            device_id=(e, lax.rem(s + d, slabs)),
            device_id_type=MESH,
        )

    densities[e] = (4.0 / (owned * energies)) * jnp.sum(out[...], axis=0, keepdims=True)
    for d in far_first(energies):
        density_copy(d).start()
    for d in range(1, energies):
        density_landing(d).wait_recv()
    density = CHARGE * jnp.sum(densities[...], axis=0)

    index = jnp.concatenate(blocks(tile_map), axis=0)

    def spread(part):
        table = jnp.broadcast_to(density[:, part * width : (part + 1) * width], (3 * tall, width))
        return jnp.take_along_axis(table, index & (width - 1), axis=1)

    source = jnp.where(inside, jnp.where(index < width, spread(0), spread(1)), 0.0)
    second = ANISO * beside(source)[tall : 2 * tall] + stencil[...]
    source = source[tall : 2 * tall]
    for d in middle_first(slabs):
        weighted[d] = tables[d, 0:1, :] * source + tables[d, 1:2, :] * second
        plane_copy(d).start()
    total = tables[0, 0:1, :] * source + tables[0, 1:2, :] * second
    for d in range(1, slabs):
        plane_copy(d).wait_recv()
        total = total + landed[d]
    potential_out[0] = total
    lax.fori_loop(0, owned * chunks, settle, 0)
    for side in ("right", "above", "below"):

        @pl.when(has[side])
        def _():
            fact_copy(side).wait_send()

    for d in range(1, energies):
        density_copy(d).wait_send()
    for d in range(1, slabs):
        plane_copy(d).wait_send()


def advance(axis_sizes, green, hopping, onsite, coupling, damping, occupation, tile_map, previous, tables):
    energies, slabs = axis_sizes
    size = hopping.shape[-1]
    count = 2 * (size // ROWS)
    tall, width = tile_map.shape[1] // energies, tile_map.shape[2]
    dma, vmem = pltpu.SemaphoreType.DMA, pl.BlockSpec(memory_space=pltpu.VMEM)
    local = (hopping, onsite, coupling, damping, occupation, tile_map, previous)
    return pl.pallas_call(
        functools.partial(step_kernel, axis_sizes),
        out_shape=(
            jax.ShapeDtypeStruct((2, size), F32),
            jax.ShapeDtypeStruct((1, tall, width), F32),
        ),
        in_specs=[pl.BlockSpec(memory_space=pl.ANY)] * 9,
        out_specs=(vmem, vmem),
        scratch_shapes=[
            *(pltpu.VMEM(array.shape, array.dtype) for array in local),
            pltpu.VMEM(tables.shape[1:], F32),
            dma((8,)),
            pltpu.VMEM((count, 2, ROWS, size), F32),
            pltpu.VMEM((count, 2, ROWS, size), F32),
            pltpu.VMEM((3, 2, 2, size, size), F32),
            pltpu.VMEM((count, 2, ROWS, size), F32),
            pltpu.VMEM((4, 8, size), F32),
            pltpu.VMEM((size, 128), F32),
            pltpu.VMEM((2, size, size), F32),
            pltpu.VMEM((4, size, size), F32),
            pltpu.VMEM((tall, width), F32),
            pltpu.VMEM((energies, 1, size), F32),
            pltpu.VMEM((slabs, tall, width), F32),
            pltpu.VMEM((slabs, tall, width), F32),
            dma((2, count)),
            dma((2, count)),
            dma((2, count)),
            dma((2, count)),
            dma((count,)),
            dma((count,)),
            dma((3,)),
            dma((3,)),
            dma((energies,)),
            dma((energies,)),
            dma((slabs,)),
            dma((slabs,)),
        ],
        compiler_params=pltpu.CompilerParams(
            collective_id=0, has_side_effects=True, vmem_limit_bytes=60 << 20
        ),
        name="step",
    )(green, hopping, onsite, coupling, damping, occupation, tile_map, previous, tables)


def solution(mesh):
    axis_sizes = (mesh.shape["energy"], mesh.shape["slab"])
    tables = line_tables(axis_sizes[1])

    def per_device(onsite, hopping, coupling, green, damping, occupation, tile_map, previous):
        lesser, potential = advance(
            axis_sizes,
            green,
            hopping,
            onsite,
            coupling,
            damping,
            occupation,
            tile_map,
            previous,
            jnp.asarray(tables),
        )

        def finish(a, b, c, d):
            c[0] = a[...]
            d[...] = b[...]

        return tuple(
            pl.pallas_call(
                finish,
                out_shape=(
                    jax.ShapeDtypeStruct((1, *lesser.shape), F32),
                    jax.ShapeDtypeStruct(potential.shape, F32),
                ),
                name="finish",
            )(lesser, potential)
        )

    in_specs = (
        P("slab", None),
        P("slab", None, None),
        P("slab", None),
        P(None, "slab", "energy", None, None),
        P("slab", "energy"),
        P("slab", "energy"),
        P("slab", None, None),
        P("slab", None, None),
    )
    out_specs = (P("slab", "energy", None), P("slab", "energy", None))
    return jax.shard_map(
        per_device, mesh=mesh, in_specs=in_specs, out_specs=out_specs, check_vma=False
    )
```

```python
import functools

import jax
import jax.numpy as jnp
import numpy as np
from jax import lax
from jax.experimental import pallas as pl
from jax.experimental.pallas import tpu as pltpu
from jax.sharding import PartitionSpec as P

F32 = jnp.float32
BF16 = jnp.bfloat16
MESH = pl.DeviceIdType.MESH
PHONON = 0.5
CHARGE = 2.0
ANISO = 0.05
SCREEN = 0.05
LAG = 3
WINDOW = 5
ROWS = 32


def line_tables(count):
    main = 2.0 + 4.0 * ANISO + SCREEN
    matrix = main * np.eye(count) - np.eye(count, k=1) - np.eye(count, k=-1)
    inverse = np.linalg.inv(matrix)
    around = (np.arange(count)[:, None] + np.arange(count)[None, :]) % count
    rows = np.arange(count)[:, None]
    weights = np.stack([inverse[rows, around], (inverse @ inverse)[rows, around]], axis=-1)
    return np.repeat(weights[..., None], 128, axis=-1).astype(np.float32)


def far_first(count):
    return sorted(range(1, count), key=lambda d: -min(d % (count // 2), -d % (count // 2)))


def middle_first(count):
    return sorted(range(1, count), key=lambda d: abs(d - count // 2))


def halves(value):
    high = value.astype(BF16)
    return high, (value - high.astype(F32)).astype(BF16)


def split(real, imag):
    return halves(real), halves(imag), halves(real + imag)


def times(first, second, turned):
    contract = (((1,), (1,)), ((), ())) if turned else (((1,), (0,)), ((), ()))

    def dot(a, b):
        return lax.dot_general(a, b, contract, preferred_element_type=F32)

    return dot(first[0], second[0]) + dot(first[0], second[1]) + dot(first[1], second[0])


def product(left, right, turned=False):
    one = times(left[0], right[0], turned)
    two = times(left[1], right[1], turned)
    both = times(left[2], right[2], turned)
    return one - two, both - one - two


def step_kernel(
    axis_sizes,
    green,
    hopping_hbm,
    onsite_hbm,
    coupling_hbm,
    damping_hbm,
    occupation_hbm,
    tile_map_hbm,
    previous_hbm,
    tables_hbm,
    out,
    potential_out,
    hopping,
    onsite,
    coupling,
    damping,
    occupation,
    tile_map,
    previous,
    tables,
    load,
    from_left,
    from_right,
    self_energy,
    relay,
    facts,
    columns,
    block,
    phonon,
    stencil,
    densities,
    weighted,
    landed,
    slab_send,
    slab_recv,
    energy_send,
    energy_recv,
    relay_recv,
    forward_send,
    fact_send,
    fact_recv,
    density_send,
    density_recv,
    plane_send,
    plane_recv,
):
    energies, slabs = axis_sizes
    e, s = lax.axis_index("energy"), lax.axis_index("slab")
    here = hopping.shape[-1]
    chunks = here // ROWS
    owned = 2
    half = energies // 2
    has = {
        "left": s > 0,
        "right": s < slabs - 1,
        "below": e > 0,
        "above": e < energies - 1,
    }
    device = {"left": (e, s - 1), "right": (e, s + 1), "below": (e - 1, s), "above": (e + 1, s)}
    crosses = {"above": e == half - 1, "below": e == half}

    def route(c):
        return lax.rem(owned * chunks - 1 - c, 3)

    def relays(side, c):
        return (route(c) > 0) & (e == (energies - route(c) if side == "above" else route(c) - 1))


    barrier = pltpu.get_barrier_semaphore()
    for d in far_first(energies):
        pl.semaphore_signal(
            barrier, inc=1, device_id=(lax.rem(e + d, energies), s), device_id_type=MESH
        )
    for d in middle_first(slabs):
        pl.semaphore_signal(
            barrier, inc=1, device_id=(e, lax.rem(s + d, slabs)), device_id_type=MESH
        )

    def loads():
        pairs = (
            (coupling_hbm, coupling),
            (damping_hbm, damping),
            (occupation_hbm, occupation),
            (onsite_hbm, onsite),
            (previous_hbm, previous),
            (tile_map_hbm, tile_map),
            (hopping_hbm, hopping),
            (tables_hbm.at[s], tables),
        )
        return [pltpu.make_async_copy(a, b, load.at[i]) for i, (a, b) in enumerate(pairs)]

    for copy in loads():
        copy.start()
    for copy in loads():
        copy.wait()

    facts[3, 0:1, :] = coupling[...]
    for k in range(owned):
        facts[3, 1 + k : 2 + k, :] = jnp.broadcast_to(damping[:, k : k + 1], (1, here))
        facts[3, 3 + k : 4 + k, :] = jnp.broadcast_to(occupation[:, k : k + 1], (1, here))

    pl.semaphore_wait(barrier, energies + slabs - 2)

    def slab_copy(side, c):
        k, row = c // chunks, pl.multiple_of(lax.rem(c, chunks) * ROWS, ROWS)
        index = 0 if side == "right" else 1
        landing = from_left if side == "right" else from_right
        return pltpu.make_async_remote_copy(
            src_ref=green.at[:, 0, k, pl.ds(row, ROWS), :],
            dst_ref=landing.at[c],
            send_sem=slab_send.at[index, c],
            recv_sem=slab_recv.at[index, c],
            device_id=device[side],
            device_id_type=MESH,
        )

    def energy_copy(side, c):
        k, row = c // chunks, pl.multiple_of(lax.rem(c, chunks) * ROWS, ROWS)
        index = 0 if side == "above" else 1
        return pltpu.make_async_remote_copy(
            src_ref=self_energy.at[0, k, :, pl.ds(row, ROWS), :],
            dst_ref=self_energy.at[1 + index, k, :, pl.ds(row, ROWS), :],
            send_sem=energy_send.at[index, c],
            recv_sem=energy_recv.at[index, c],
            device_id=device[side],
            device_id_type=MESH,
        )

    def relay_copy(side, c):
        k, row = c // chunks, pl.multiple_of(lax.rem(c, chunks) * ROWS, ROWS)
        index = 0 if side == "above" else 1
        return pltpu.make_async_remote_copy(
            src_ref=self_energy.at[0, k, :, pl.ds(row, ROWS), :],
            dst_ref=relay.at[c],
            send_sem=energy_send.at[index, c],
            recv_sem=relay_recv.at[c],
            device_id=(energies - route(c) if side == "above" else route(c) - 1, s),
            device_id_type=MESH,
        )

    def forward_copy(side, c):
        k, row = c // chunks, pl.multiple_of(lax.rem(c, chunks) * ROWS, ROWS)
        index = 0 if side == "above" else 1
        return pltpu.make_async_remote_copy(
            src_ref=relay.at[c],
            dst_ref=self_energy.at[1 + index, k, :, pl.ds(row, ROWS), :],
            send_sem=forward_send.at[c],
            recv_sem=energy_recv.at[index, c],
            device_id=(half if side == "above" else half - 1, s),
            device_id_type=MESH,
        )

    def forward(c):
        for side in ("above", "below"):

            @pl.when(relays(side, c))
            def _():
                relay_copy(side, c).wait_recv()
                forward_copy(side, c).start()

    def fact_copy(side):
        index = {"right": 0, "above": 1, "below": 2}[side]
        return pltpu.make_async_remote_copy(
            src_ref=facts.at[3],
            dst_ref=facts.at[index],
            send_sem=fact_send.at[index],
            recv_sem=fact_recv.at[index],
            device_id=device[side],
            device_id_type=MESH,
        )

    @pl.when(has["right"])
    def _():
        fact_copy("right").start()

    def send_green(c, carry):
        @pl.when(has["right"])
        def _():
            slab_copy("right", c).start()

        @pl.when(has["left"])
        def _():
            slab_copy("left", c).start()

        return carry

    lax.fori_loop(0, WINDOW, send_green, 0)

    for side in ("above", "below"):

        @pl.when(has[side])
        def _():
            fact_copy(side).start()

    tall = potential_out.shape[1]
    width = potential_out.shape[2]

    def blocks(ref):
        own = ref[0, pl.ds(pl.multiple_of(e * tall, tall), tall), :]
        before = ref[0, pl.ds(pl.multiple_of(jnp.maximum(e - 1, 0) * tall, tall), tall), :]
        after = ref[
            0, pl.ds(pl.multiple_of(jnp.minimum(e + 1, energies - 1) * tall, tall), tall), :
        ]
        return before, own, after

    cell = lax.broadcasted_iota(jnp.int32, (3 * tall, width), 1)
    line = lax.broadcasted_iota(jnp.int32, (3 * tall, width), 0) + (e - 1) * tall
    inside = (line >= 0) & (line < energies * tall)

    def beside(field):
        up = pltpu.roll(field, 1, 0)
        down = pltpu.roll(field, 3 * tall - 1, 0)
        left = jnp.where(cell == 0, 0.0, pltpu.roll(field, 1, 1))
        right = jnp.where(cell == width - 1, 0.0, pltpu.roll(field, width - 1, 1))
        return up + down + left + right

    potential = jnp.where(inside, jnp.concatenate(blocks(previous), axis=0), 0.0)
    potential = jnp.where(inside, beside(potential), 0.0)
    stencil[...] = (ANISO * ANISO) * beside(potential)[tall : 2 * tall]

    rows = lax.broadcasted_iota(jnp.int32, (here, here), 0)
    lanes = lax.broadcasted_iota(jnp.int32, (here, here), 1)

    def column(row):
        return jnp.sum(jnp.where(rows == lanes, row, 0.0), axis=1, keepdims=True)

    columns[:, 0:1] = column(onsite[...])
    columns[:, 1:2] = column(coupling[...])

    @pl.when(jnp.logical_not(has["left"]))
    def _():
        from_left[...] = jnp.zeros_like(from_left)
        facts[0] = jnp.zeros_like(facts[0])

    @pl.when(jnp.logical_not(has["right"]))
    def _():
        from_right[...] = jnp.zeros_like(from_right)

    @pl.when(has["left"])
    def _():
        fact_copy("right").wait_recv()

    columns[:, 2:3] = column(facts[0, 0:1, :])

    def form_self_energy(c, carry):
        k, row = c // chunks, pl.multiple_of(lax.rem(c, chunks) * ROWS, ROWS)

        @pl.when(has["left"])
        def _():
            slab_copy("right", c).wait_recv()

        @pl.when(has["right"])
        def _():
            slab_copy("left", c).wait_recv()

        @pl.when(c + WINDOW < owned * chunks)
        def _():
            send_green(c + WINDOW, 0)

        weight_left = columns[pl.ds(row, ROWS), 2:3] * facts[0, 0:1, :]
        weight_right = columns[pl.ds(row, ROWS), 1:2] * facts[3, 0:1, :]
        for part in range(2):
            self_energy[0, k, part, pl.ds(row, ROWS), :] = (
                weight_left * from_left[c, part] + weight_right * from_right[c, part]
            )
        for side in ("above", "below"):

            bent = crosses[side] & (route(c) > 0)

            @pl.when(has[side] & jnp.logical_not(bent))
            def _():
                energy_copy(side, c).start()

            @pl.when(bent)
            def _():
                relay_copy(side, c).start()

        @pl.when(c >= LAG)
        def _():
            forward(c - LAG)

        return carry

    def diagonal_inverse(energy, level, damp):
        real = energy - level
        modulus = real * real + damp * damp
        return real / modulus, -damp / modulus

    def step(t, carry):
        k, kind = t // 3, lax.rem(t, 3)
        lax.fori_loop(
            jnp.where(t == 0, 0, jnp.minimum(12 + 2 * t, owned * chunks)),
            jnp.minimum(14 + 2 * t, owned * chunks),
            form_self_energy,
            0,
        )

        @pl.when(t == 2)
        def _():
            forward(owned * chunks - 3)
            forward(owned * chunks - 2)
            forward(owned * chunks - 1)

        side = jnp.where(lax.rem(e, half) >= half // 2, kind, 1 - kind)
        slot = jnp.where(kind == 2, 0, 1 + side)
        fact = jnp.where(kind == 2, 3, 1 + side)
        present = (kind == 2) | (jnp.where(side == 0, e, energies - 1 - e) > 0)

        def arrive(side):
            def one(c, inner):
                energy_copy(side, c).wait_recv()
                return inner

            lax.fori_loop(k * chunks, (k + 1) * chunks, one, 0)

            @pl.when(k == 0)
            def _():
                fact_copy(side).wait_recv()

        @pl.when((kind < 2) & (side == 0) & has["below"])
        def _():
            arrive("above")

        @pl.when((kind < 2) & (side == 1) & has["above"])
        def _():
            arrive("below")

        @pl.when(kind == 0)
        def _():
            phonon[...] = jnp.zeros_like(phonon)

        @pl.when(present)
        def _():
            place = owned * (e + jnp.where(kind == 2, 0, 2 * side - 1)) + k
            energy = -2.0 + 4.0 * (place.astype(F32) + 0.5) / (owned * energies)
            damp = facts[fact, pl.ds(1 + k, 1), :]
            x_real, x_imag = diagonal_inverse(energy, onsite[...], damp)
            se_real, se_imag = self_energy[slot, k, 0], self_energy[slot, k, 1]

            @pl.when(kind < 2)
            def _():
                block[0] = hopping[0] + se_real
                block[1] = se_imag

            @pl.when(kind == 2)
            def _():
                block[0] = hopping[0] + se_real + phonon[0]
                block[1] = se_imag + phonon[1]

            h_real, h_imag = block[0], block[1]
            a_real = h_real * x_real - h_imag * x_imag
            a_imag = h_real * x_imag + h_imag * x_real
            a = split(a_real, a_imag)
            square = product(a, a)
            two = split(*square)
            cube = product(a, two)
            fourth = product(two, two)
            t_real = a_real + square[0] + cube[0]
            t_imag = a_imag + square[1] + cube[1]
            rest = product(split(t_real, t_imag), split(*fourth))
            t_real = t_real + fourth[0] + rest[0]
            t_imag = t_imag + fourth[1] + rest[1]
            series = split(t_real, t_imag)

            fill = facts[fact, pl.ds(3 + k, 1), :]
            sigma_real = -fill * (se_real - se_real.T)
            sigma_imag = -fill * (se_imag + se_imag.T)

            @pl.when(kind < 2)
            def _():
                more = product(series, split(sigma_real, sigma_imag))
                w_real, w_imag = sigma_real + more[0], sigma_imag + more[1]
                adjoint = (series[0], halves(-t_imag), halves(t_real - t_imag))
                more = product(split(w_real, w_imag), adjoint, True)
                u_real, u_imag = w_real + more[0], w_imag + more[1]
                c_real, c_imag = diagonal_inverse(energy, columns[:, 0:1], damp[:, 0:1])
                c_real, c_imag = PHONON * c_real, PHONON * c_imag
                v_real = c_real * u_real - c_imag * u_imag
                v_imag = c_real * u_imag + c_imag * u_real
                unit = jnp.where(rows == lanes, 1.0, 0.0)
                g_real = unit + t_real
                phonon[0] += c_real * g_real - c_imag * t_imag
                phonon[1] += c_real * t_imag + c_imag * g_real
                phonon[2] += v_real * x_real + v_imag * x_imag
                phonon[3] += v_imag * x_real - v_real * x_imag

            @pl.when(kind == 2)
            def _():
                mixed_real = sigma_real + phonon[2]
                mixed_imag = sigma_imag + phonon[3]
                more = product(series, split(mixed_real, mixed_imag))
                w_real, w_imag = mixed_real + more[0], mixed_imag + more[1]
                terms = w_imag * t_real - w_real * t_imag + jnp.where(rows == lanes, w_imag, 0.0)
                total = jnp.sum(terms.T, axis=0, keepdims=True)
                out[pl.ds(k, 1), :] = (x_real * x_real + x_imag * x_imag) * total

        return carry

    lax.fori_loop(0, 3 * owned, step, 0)

    def settle(c, carry):
        for side in ("right", "left"):

            @pl.when(has[side])
            def _():
                slab_copy(side, c).wait_send()

        for side in ("above", "below"):

            @pl.when(has[side])
            def _():
                energy_copy(side, c).wait_send()

        @pl.when(relays("above", c) | relays("below", c))
        def _():
            forward_copy("above", c).wait_send()

        return carry

    def density_copy(d):
        return pltpu.make_async_remote_copy(
            src_ref=densities.at[e],
            dst_ref=densities.at[e],
            send_sem=density_send.at[d],
            recv_sem=density_recv.at[d],
            device_id=(lax.rem(e + d, energies), s),
            device_id_type=MESH,
        )

    def density_landing(d):
        slot = lax.rem(e + energies - d, energies)
        return pltpu.make_async_remote_copy(
            src_ref=densities.at[slot],
            dst_ref=densities.at[slot],
            send_sem=density_send.at[d],
            recv_sem=density_recv.at[d],
            device_id=(lax.rem(e + d, energies), s),
            device_id_type=MESH,
        )

    def plane_copy(d):
        return pltpu.make_async_remote_copy(
            src_ref=weighted.at[d],
            dst_ref=landed.at[d],
            send_sem=plane_send.at[d],
            recv_sem=plane_recv.at[d],
            device_id=(e, lax.rem(s + d, slabs)),
            device_id_type=MESH,
        )

    densities[e] = (4.0 / (owned * energies)) * jnp.sum(out[...], axis=0, keepdims=True)
    for d in far_first(energies):
        density_copy(d).start()
    for d in range(1, energies):
        density_landing(d).wait_recv()
    density = CHARGE * jnp.sum(densities[...], axis=0)

    index = jnp.concatenate(blocks(tile_map), axis=0)

    def spread(part):
        table = jnp.broadcast_to(density[:, part * width : (part + 1) * width], (3 * tall, width))
        return jnp.take_along_axis(table, index & (width - 1), axis=1)

    source = jnp.where(inside, jnp.where(index < width, spread(0), spread(1)), 0.0)
    second = ANISO * beside(source)[tall : 2 * tall] + stencil[...]
    source = source[tall : 2 * tall]
    for d in middle_first(slabs):
        weighted[d] = tables[d, 0:1, :] * source + tables[d, 1:2, :] * second
        plane_copy(d).start()
    total = tables[0, 0:1, :] * source + tables[0, 1:2, :] * second
    for d in range(1, slabs):
        plane_copy(d).wait_recv()
        total = total + landed[d]
    potential_out[0] = total
    lax.fori_loop(0, owned * chunks, settle, 0)
    for side in ("right", "above", "below"):

        @pl.when(has[side])
        def _():
            fact_copy(side).wait_send()

    for d in range(1, energies):
        density_copy(d).wait_send()
    for d in range(1, slabs):
        plane_copy(d).wait_send()


def advance(axis_sizes, green, hopping, onsite, coupling, damping, occupation, tile_map, previous, tables):
    energies, slabs = axis_sizes
    size = hopping.shape[-1]
    count = 2 * (size // ROWS)
    tall, width = tile_map.shape[1] // energies, tile_map.shape[2]
    dma, vmem = pltpu.SemaphoreType.DMA, pl.BlockSpec(memory_space=pltpu.VMEM)
    local = (hopping, onsite, coupling, damping, occupation, tile_map, previous)
    return pl.pallas_call(
        functools.partial(step_kernel, axis_sizes),
        out_shape=(
            jax.ShapeDtypeStruct((2, size), F32),
            jax.ShapeDtypeStruct((1, tall, width), F32),
        ),
        in_specs=[pl.BlockSpec(memory_space=pl.ANY)] * 9,
        out_specs=(vmem, vmem),
        scratch_shapes=[
            *(pltpu.VMEM(array.shape, array.dtype) for array in local),
            pltpu.VMEM(tables.shape[1:], F32),
            dma((8,)),
            pltpu.VMEM((count, 2, ROWS, size), F32),
            pltpu.VMEM((count, 2, ROWS, size), F32),
            pltpu.VMEM((3, 2, 2, size, size), F32),
            pltpu.VMEM((count, 2, ROWS, size), F32),
            pltpu.VMEM((4, 8, size), F32),
            pltpu.VMEM((size, 128), F32),
            pltpu.VMEM((2, size, size), F32),
            pltpu.VMEM((4, size, size), F32),
            pltpu.VMEM((tall, width), F32),
            pltpu.VMEM((energies, 1, size), F32),
            pltpu.VMEM((slabs, tall, width), F32),
            pltpu.VMEM((slabs, tall, width), F32),
            dma((2, count)),
            dma((2, count)),
            dma((2, count)),
            dma((2, count)),
            dma((count,)),
            dma((count,)),
            dma((3,)),
            dma((3,)),
            dma((energies,)),
            dma((energies,)),
            dma((slabs,)),
            dma((slabs,)),
        ],
        compiler_params=pltpu.CompilerParams(
            collective_id=0, has_side_effects=True, vmem_limit_bytes=60 << 20
        ),
        name="step",
    )(green, hopping, onsite, coupling, damping, occupation, tile_map, previous, tables)


def solution(mesh):
    axis_sizes = (mesh.shape["energy"], mesh.shape["slab"])
    tables = line_tables(axis_sizes[1])

    def per_device(onsite, hopping, coupling, green, damping, occupation, tile_map, previous):
        lesser, potential = advance(
            axis_sizes,
            green,
            hopping,
            onsite,
            coupling,
            damping,
            occupation,
            tile_map,
            previous,
            jnp.asarray(tables),
        )

        def finish(a, b, c, d):
            c[0] = a[...]
            d[...] = b[...]

        return tuple(
            pl.pallas_call(
                finish,
                out_shape=(
                    jax.ShapeDtypeStruct((1, *lesser.shape), F32),
                    jax.ShapeDtypeStruct(potential.shape, F32),
                ),
                name="finish",
            )(lesser, potential)
        )

    in_specs = (
        P("slab", None),
        P("slab", None, None),
        P("slab", None),
        P(None, "slab", "energy", None, None),
        P("slab", "energy"),
        P("slab", "energy"),
        P("slab", None, None),
        P("slab", None, None),
    )
    out_specs = (P("slab", "energy", None), P("slab", "energy", None))
    return jax.shard_map(
        per_device, mesh=mesh, in_specs=in_specs, out_specs=out_specs, check_vma=False
    )
```
